32 devices in a mesh: shard: 8 (over z, x), rep: 4 (over y, core).
Axes of the slice: x: 2, y: 2, z: 4, core: 2. Of those that a mesh axis runs over, the one named last changes fastest.
Arguments:
- images: bfloat16 [32, 197, 768], P(('shard', 'rep')), may hold values from -6 to 6
- cotangent: bfloat16 [32, 197, 768], P(('shard', 'rep')), may hold values from -6 to 6
- weights_in: float32 [768, 6144], P('shard'), may hold values from -13 to 13
- weights_down: float32 [3072, 768], P('shard'), may hold values from -0.109375 to 0.109375
- vectors: float32 [12, 768], P(None, 'shard'), may hold values from -1.5 to 1.5, as said below
- mean_in: float32 [768, 6144], P('shard'), may hold values from -256 to 256
- mean_down: float32 [3072, 768], P('shard'), may hold values from -256 to 256
- mean_vectors: float32 [12, 768], P(None, 'shard'), may hold values from -256 to 256
- square_in: float32 [768, 6144], P('shard'), may hold values from 63.04 to 6304
- square_down: float32 [3072, 768], P('shard'), may hold values from 63.04 to 6304
- square_vectors: float32 [12, 768], P(None, 'shard'), may hold values from 63.04 to 6304
Outputs:
- block_out: bfloat16 [32, 197, 768], P(('shard', 'rep'))
- input_grad: float32 [32, 197, 768], P(('shard', 'rep'))
- grad_in: float32 [768, 6144], P('shard')
- grad_down: float32 [3072, 768], P('shard')
- grad_vectors: float32 [12, 768], P(None, 'shard')
- updated_in: float32 [768, 6144], P('shard')
- updated_down: float32 [3072, 768], P('shard')
- updated_vectors: float32 [12, 768], P(None, 'shard')
- next_mean_in: float32 [768, 6144], P('shard')
- next_mean_down: float32 [3072, 768], P('shard')
- next_mean_vectors: float32 [12, 768], P(None, 'shard')
- next_square_in: float32 [768, 6144], P('shard')
- next_square_down: float32 [3072, 768], P('shard')
- next_square_vectors: float32 [12, 768], P(None, 'shard')
The draws below stay inside these ranges and needn't reach their ends.
Inputs may be any that keep to these rules, and one draw needn't show every extreme that they name: `vectors`: rows 0 and 5 are the norms' gains.
All inputs are finite; a program needn't handle non-finite values.
Results may differ from the reference program's by a relative error of at most 0.023.
Values may be sent and summed in bfloat16 or wider, within the bound.
A program may use at most 128 MiB of HBM per device.

```python
import math
import jax
import jax.numpy as jnp
from jax import lax

D = 768
FF = 3072
HEADS = 12
SEQ = 197
IMG_DEV = 1
IMAGES = 32


def truncated(key_piece, shape_of, spread):
    return spread * jax.random.truncated_normal(key_piece, -4.0, 4.0, shape_of, jnp.float32)


def draw_weights_in(key, part):
    subkeys = jax.random.split(key, 5)
    spread = D ** (-0.5)
    queries = truncated(subkeys[0], (D, D), spread)
    keys_part = truncated(subkeys[1], (D, D), spread)
    values_part = truncated(subkeys[2], (D, D), spread)
    output_part = truncated(subkeys[3], (D, D), 4.0 * spread)
    upward_part = truncated(subkeys[4], (D, FF), spread)
    return jnp.concatenate([queries, keys_part, values_part, output_part, upward_part], axis=1)


def draw_vectors(key, part):
    subkeys = jax.random.split(key, 2)
    gain_values = jax.random.uniform(subkeys[0], (12, D), jnp.float32, 0.5, 1.5)
    shift_values = truncated(subkeys[1], (12, D), 0.3)
    row_index = jnp.arange(12)[:, None]
    is_gain = ((row_index == 0) | (row_index == 5)).astype(jnp.float32)
    return is_gain * gain_values + (1.0 - is_gain) * shift_values


def with_spikes(drawn, key, source, target, blocks, factor):
    def block_of(dim):
        return (jnp.arange(drawn.shape[dim]) // (drawn.shape[dim] // blocks)).reshape((-1,) + (1,) * (drawn.ndim - 1 - dim))

    first = jax.random.permutation(key, blocks)[block_of(target)]
    second = (block_of(target) + blocks // 2) % blocks
    return jnp.where((block_of(source) == first) | (block_of(source) == second), factor * drawn, drawn)


def shard_levels(key, shape, cuts, least, top_value):
    def one(position, parts):
        steps = jax.random.uniform(jax.random.fold_in(jax.random.fold_in(key, 6), position), (parts,), jnp.float32, least / len(cuts), top_value / len(cuts))
        return jnp.repeat(jnp.exp(steps), shape[position] // parts).reshape((-1,) + (1,) * (len(shape) - position - 1))

    level = one(*cuts[0])
    for cut in cuts[1:]:
        level = level * one(*cut)
    return level


def bell_draw(stream_key, shape, deviation, most, cuts=(), dtype=jnp.bfloat16):
    entries = deviation * jax.random.normal(stream_key, shape, jnp.float32)
    if cuts:
        entries = entries * shard_levels(stream_key, shape, cuts, -0.22, 0.18)
    return jnp.clip(entries, -most, most).astype(dtype)


def heavy_noise(own_key, extent, deviation, most, cuts, heavy, held_as=jnp.bfloat16):
    array = deviation * jax.random.normal(own_key, extent, jnp.float32)
    if cuts:
        array = array * shard_levels(own_key, extent, cuts, -0.22, 0.18)
    return jnp.clip(with_spikes(array, jax.random.fold_in(own_key, 3), *heavy), -most, most).astype(held_as)


def setup_inputs(seed: int = 0) -> dict:
    key_list = jax.random.split(jax.random.key(seed), 12)
    images = bell_draw(key_list[0], (IMAGES, SEQ, D), 1.0, 6.0, ((0, 32),))
    cotangent = heavy_noise(key_list[1], (IMAGES, SEQ, D), 1.0, 6.0, ((0, 32),), (0, 2, 32, 2.75))
    weights_in = draw_weights_in(jax.random.fold_in(key_list[11], 71), 0)
    weights_down = bell_draw(key_list[3], (FF, D), FF ** -0.5, 0.109375, ((0, 8),), jnp.float32)
    vectors = draw_vectors(jax.random.fold_in(key_list[11], 71), 0)
    mean_in = bell_draw(key_list[5], (D, 4 * D + FF), ((IMAGES * SEQ) ** 0.5 * 0.5), 256.0, ((0, 8),), jnp.float32)
    mean_down = bell_draw(key_list[6], (FF, D), ((IMAGES * SEQ) ** 0.5 * 0.5), 256.0, ((0, 8),), jnp.float32)
    mean_vectors = bell_draw(key_list[7], (12, D), ((IMAGES * SEQ) ** 0.5 * 0.5), 256.0, ((1, 8),), jnp.float32)
    square_in = jnp.clip(jnp.exp(math.log(6304.0) - 4.6051702 * jax.random.uniform(key_list[8], (D, 4 * D + FF), jnp.float32) ** shard_levels(key_list[8], (D, 4 * D + FF), ((0, 8),), -0.2, 0.2)), 63.04, 6304.0)
    square_down = jnp.clip(jnp.exp(math.log(6304.0) - 4.6051702 * jax.random.uniform(key_list[9], (FF, D), jnp.float32) ** shard_levels(key_list[9], (FF, D), ((0, 8),), -0.2, 0.2)), 63.04, 6304.0)
    square_vectors = jnp.clip(jnp.exp(math.log(6304.0) - 4.6051702 * jax.random.uniform(key_list[10], (12, D), jnp.float32) ** shard_levels(key_list[10], (12, D), ((1, 8),), -0.2, 0.2)), 63.04, 6304.0)
    return {"images": images, "cotangent": cotangent, "weights_in": weights_in, "weights_down": weights_down, "vectors": vectors, "mean_in": mean_in, "mean_down": mean_down, "mean_vectors": mean_vectors, "square_in": square_in, "square_down": square_down, "square_vectors": square_vectors}


NORM_EPS = 1e-06
BETA_ONE = 0.9
BETA_TWO = 0.95
ADAM_EPS = 1e-08
RATE_MATRIX = 0.008
RATE_VECTOR = 0.15
DECAY_MATRIX = 0.05
STEP_COUNT = 2.0

def to_half(array_in):
    return array_in.astype(jnp.bfloat16)

def matmul(left, right):
    return jnp.dot(left, right, preferred_element_type=jnp.float32)

def times_transposed(left, right):
    return lax.dot_general(left, right, (((1,), (1,)), ((), ())), preferred_element_type=jnp.float32)

def transposed_times(left, right):
    return lax.dot_general(left, right, (((0,), (0,)), ((), ())), preferred_element_type=jnp.float32)

def layer_norm(inputs, gain, shift):
    centred = inputs - lax.optimization_barrier(jnp.mean(inputs, axis=-1, keepdims=True))
    inv_std = lax.rsqrt(lax.optimization_barrier(jnp.mean(centred * centred, axis=-1, keepdims=True)) + NORM_EPS)
    normed = centred * inv_std
    return (normed, inv_std, normed * gain + shift)

def norm_back(grad_after, normed, inv_std, gain):
    grad_normed = grad_after * gain
    grad_inputs = inv_std * (grad_normed - lax.optimization_barrier(jnp.mean(grad_normed, axis=-1, keepdims=True)) - normed * lax.optimization_barrier(jnp.mean(grad_normed * normed, axis=-1, keepdims=True)))
    return (grad_inputs, lax.optimization_barrier(jnp.sum(grad_after * normed, axis=0)), lax.optimization_barrier(jnp.sum(grad_after, axis=0)))

def gaussian_unit(hidden):
    cdf_part = 0.5 * (1.0 + jax.scipy.special.erf(hidden * 0.7071067811865476))
    slope = cdf_part + hidden * jnp.exp(-0.5 * hidden * hidden) * 0.3989422804014327
    return (hidden * cdf_part, slope)

def head_scores(query_heads, key_heads, score_scale):
    return jnp.einsum('bqhe,bkhe->bhqk', query_heads.astype(jnp.float32), key_heads.astype(jnp.float32)) * score_scale

def block_pass(images, cotangent, matrix_half, down_half, vector_half):
    img_count, seq_len, model_width = images.shape
    head_dim = model_width // HEADS
    score_scale = 1.0 / math.sqrt(head_dim)
    row_count = img_count * seq_len
    head_shape = (img_count, seq_len, HEADS, head_dim)
    vector_float = vector_half.astype(jnp.float32)
    joint_weights = matrix_half[:, :3 * model_width]
    output_weights = matrix_half[:, 3 * model_width:4 * model_width]
    upward_weights = matrix_half[:, 4 * model_width:]
    flat_in = images.reshape(row_count, model_width).astype(jnp.float32)
    normed_one, inv_one, pre_one = layer_norm(flat_in, vector_float[0], vector_float[1])
    act_one = to_half(pre_one)
    projected = matmul(act_one, joint_weights)
    query_heads = to_half(projected[:, :model_width] + vector_float[2]).reshape(head_shape)
    key_heads = to_half(projected[:, model_width:2 * model_width]).reshape(head_shape)
    value_heads = to_half(projected[:, 2 * model_width:] + vector_float[3]).reshape(head_shape)
    scores = head_scores(query_heads, key_heads, score_scale)
    log_total = jax.nn.logsumexp(scores, axis=-1, keepdims=True)
    probs_half = to_half(jnp.exp(scores - log_total))
    attended = to_half(jnp.einsum('bhqk,bkhe->bqhe', probs_half.astype(jnp.float32), value_heads.astype(jnp.float32)).reshape(row_count, model_width))
    hidden_one = flat_in + matmul(attended, output_weights) + vector_float[4]
    normed_two, inv_two, pre_two = layer_norm(hidden_one, vector_float[5], vector_float[6])
    act_two = to_half(pre_two)
    up_input = matmul(act_two, upward_weights) + vector_float[8:].reshape(-1)
    gelu_out, gelu_slope = gaussian_unit(up_input)
    gelu_half = to_half(gelu_out)
    block_out = to_half(hidden_one + matmul(gelu_half, down_half) + vector_float[7])
    grad_half = cotangent.reshape(row_count, model_width)
    grad_out = grad_half.astype(jnp.float32)
    grad_up = times_transposed(grad_half, down_half) * gelu_slope
    up_half = to_half(grad_up)
    grad_act_two = times_transposed(up_half, upward_weights)
    grad_norm_two, grad_gain_two, grad_shift_two = norm_back(grad_act_two, normed_two, inv_two, vector_float[5])
    grad_hidden = grad_out + grad_norm_two
    hidden_half = to_half(grad_hidden)
    grad_att = to_half(times_transposed(hidden_half, output_weights)).reshape(head_shape)
    prob_float = jnp.exp(head_scores(query_heads, key_heads, score_scale) - log_total)
    grad_probs = jnp.einsum('bqhe,bkhe->bhqk', grad_att.astype(jnp.float32), value_heads.astype(jnp.float32))
    row_inner = lax.optimization_barrier(jnp.sum(prob_float * grad_probs, axis=-1, keepdims=True))
    grad_scores = to_half(prob_float * (grad_probs - row_inner) * score_scale)
    grad_query = jnp.einsum('bhqk,bkhe->bqhe', grad_scores.astype(jnp.float32), key_heads.astype(jnp.float32)).reshape(row_count, model_width)
    grad_key = jnp.einsum('bhqk,bqhe->bkhe', grad_scores.astype(jnp.float32), query_heads.astype(jnp.float32)).reshape(row_count, model_width)
    grad_value = jnp.einsum('bhqk,bqhe->bkhe', probs_half.astype(jnp.float32), grad_att.astype(jnp.float32)).reshape(row_count, model_width)
    grad_proj = to_half(jnp.concatenate([grad_query, grad_key, grad_value], axis=1))
    grad_act_one = times_transposed(grad_proj, joint_weights)
    grad_norm_one, grad_gain_one, grad_shift_one = norm_back(grad_act_one, normed_one, inv_one, vector_float[0])
    input_grad = grad_hidden + grad_norm_one
    grad_in = jnp.concatenate([transposed_times(act_one, grad_proj), transposed_times(attended, hidden_half), transposed_times(act_two, up_half)], axis=1)
    grad_down = transposed_times(gelu_half, grad_half)
    small_rows = jnp.stack([grad_gain_one, grad_shift_one, lax.optimization_barrier(jnp.sum(grad_query, axis=0)), lax.optimization_barrier(jnp.sum(grad_value, axis=0)), lax.optimization_barrier(jnp.sum(grad_hidden, axis=0)), grad_gain_two, grad_shift_two, lax.optimization_barrier(jnp.sum(grad_out, axis=0))])
    grad_vectors = jnp.concatenate([small_rows, lax.optimization_barrier(jnp.sum(grad_up, axis=0)).reshape(4, model_width)], axis=0)
    return (block_out.reshape(images.shape), input_grad.reshape(images.shape), grad_in, grad_down, grad_vectors)

def adam_update(weights, first, second, gradient, rate, decay):
    next_first = BETA_ONE * first + (1.0 - BETA_ONE) * gradient
    next_second = BETA_TWO * second + (1.0 - BETA_TWO) * gradient * gradient
    corr_first = next_first / (1.0 - BETA_ONE ** STEP_COUNT)
    corr_second = next_second / (1.0 - BETA_TWO ** STEP_COUNT)
    updated = weights - rate * (corr_first / (jnp.sqrt(corr_second) + ADAM_EPS) + decay * weights)
    return (updated, next_first, next_second)

def rounded(partial_sum):
    return to_half(partial_sum).astype(jnp.float32)

def reference(images, cotangent, weights_in, weights_down, vectors, mean_in, mean_down, mean_vectors, square_in, square_down, square_vectors):
    matrix_half = to_half(weights_in)
    down_half = to_half(weights_down)
    vector_half = to_half(vectors)
    device_count = IMAGES // IMG_DEV
    grouped_in = images.reshape(device_count, IMG_DEV, SEQ, D)
    grouped_cot = cotangent.reshape(device_count, IMG_DEV, SEQ, D)

    def accumulate(totals, pieces):
        outputs = block_pass(pieces[0], pieces[1], matrix_half, down_half, vector_half)
        sums = (totals[0] + rounded(outputs[2]), totals[1] + rounded(outputs[3]), totals[2] + rounded(outputs[4]))
        return (sums, (outputs[0], outputs[1]))
    start_sums = (jnp.zeros(weights_in.shape, jnp.float32), jnp.zeros(weights_down.shape, jnp.float32), jnp.zeros(vectors.shape, jnp.float32))
    totals, stacked = lax.scan(accumulate, start_sums, (grouped_in, grouped_cot))
    block_out = stacked[0].reshape(IMAGES, SEQ, D)
    input_grad = stacked[1].reshape(IMAGES, SEQ, D)
    grad_in, grad_down, grad_vectors = totals
    new_in = adam_update(weights_in, mean_in, square_in, grad_in, RATE_MATRIX, DECAY_MATRIX)
    new_down = adam_update(weights_down, mean_down, square_down, grad_down, RATE_MATRIX, DECAY_MATRIX)
    new_vectors = adam_update(vectors, mean_vectors, square_vectors, grad_vectors, RATE_VECTOR, 0.0)
    return (block_out, input_grad, grad_in, grad_down, grad_vectors, new_in[0], new_down[0], new_vectors[0], new_in[1], new_down[1], new_vectors[1], new_in[2], new_down[2], new_vectors[2])
```

```python
import functools
import math

import jax
import jax.numpy as jnp
from jax import lax
from jax.experimental import pallas as pl
from jax.experimental.pallas import tpu as pltpu
from jax.sharding import PartitionSpec as P

HEADS = 12


NORM_EPS = 1e-06
BETA_ONE = 0.9
BETA_TWO = 0.95
ADAM_EPS = 1e-08
RATE_MATRIX = 0.008
RATE_VECTOR = 0.15
DECAY_MATRIX = 0.05
STEP_COUNT = 2.0


def to_half(array_in):
    return array_in.astype(jnp.bfloat16)


def matmul(left, right):
    return jnp.dot(left, right, preferred_element_type=jnp.float32)


def times_transposed(left, right):
    return lax.dot_general(
        left, right, (((1,), (1,)), ((), ())), preferred_element_type=jnp.float32
    )


def transposed_times(left, right):
    return lax.dot_general(
        left, right, (((0,), (0,)), ((), ())), preferred_element_type=jnp.float32
    )


def layer_norm(inputs, gain, shift):
    centred = inputs - jnp.mean(inputs, axis=-1, keepdims=True)
    inv_std = lax.rsqrt(jnp.mean(centred * centred, axis=-1, keepdims=True) + NORM_EPS)
    normed = centred * inv_std
    return (normed, inv_std, normed * gain + shift)


def norm_back(grad_after, normed, inv_std, gain):
    grad_normed = grad_after * gain
    grad_inputs = inv_std * (
        grad_normed
        - jnp.mean(grad_normed, axis=-1, keepdims=True)
        - normed * jnp.mean(grad_normed * normed, axis=-1, keepdims=True)
    )
    return (grad_inputs, jnp.sum(grad_after * normed, axis=0), jnp.sum(grad_after, axis=0))


def gaussian_unit(hidden):
    cdf_part = 0.5 * (1.0 + jax.scipy.special.erf(hidden * 0.7071067811865476))
    slope = cdf_part + hidden * jnp.exp(-0.5 * hidden * hidden) * 0.3989422804014327
    return (hidden * cdf_part, slope)


def head_scores(query_heads, key_heads, score_scale):
    return (
        jnp.einsum("bqhe,bkhe->bhqk", query_heads, key_heads, preferred_element_type=jnp.float32)
        * score_scale
    )


def forward_pass(images, matrix_half, down_half, vector_half):
    img_count, seq_len, model_width = images.shape
    head_dim = model_width // HEADS
    score_scale = 1.0 / math.sqrt(head_dim)
    row_count = img_count * seq_len
    head_shape = (img_count, seq_len, HEADS, head_dim)
    vector_float = vector_half.astype(jnp.float32)
    flat_in = images.reshape(row_count, model_width).astype(jnp.float32)
    normed_one, inv_one, pre_one = layer_norm(flat_in, vector_float[0], vector_float[1])
    act_one = to_half(pre_one)
    projected = matmul(act_one, matrix_half[:, : 3 * model_width])
    query_heads = to_half(projected[:, :model_width] + vector_float[2]).reshape(head_shape)
    key_heads = to_half(projected[:, model_width : 2 * model_width]).reshape(head_shape)
    value_heads = to_half(projected[:, 2 * model_width :] + vector_float[3]).reshape(head_shape)
    scores = head_scores(query_heads, key_heads, score_scale)
    log_total = jax.nn.logsumexp(scores, axis=-1, keepdims=True)
    probs_half = to_half(jnp.exp(scores - log_total))
    attended = to_half(
        jnp.einsum(
            "bhqk,bkhe->bqhe", probs_half, value_heads, preferred_element_type=jnp.float32
        ).reshape(row_count, model_width)
    )
    hidden_one = (
        flat_in
        + matmul(attended, matrix_half[:, 3 * model_width : 4 * model_width])
        + vector_float[4]
    )
    normed_two, inv_two, pre_two = layer_norm(hidden_one, vector_float[5], vector_float[6])
    act_two = to_half(pre_two)
    up_input = matmul(act_two, matrix_half[:, 4 * model_width :]) + vector_float[8:].reshape(-1)
    gelu_out, gelu_slope = gaussian_unit(up_input)
    gelu_half = to_half(gelu_out)
    block_out = to_half(hidden_one + matmul(gelu_half, down_half) + vector_float[7])
    saved = (
        normed_one,
        inv_one,
        act_one,
        query_heads,
        key_heads,
        value_heads,
        log_total,
        attended,
        normed_two,
        inv_two,
        act_two,
        gelu_slope,
        gelu_half,
    )
    return (block_out.reshape(images.shape), saved)


def backward_pass(cotangent, saved, matrix_half, down_half, vector_half):
    (
        normed_one,
        inv_one,
        act_one,
        query_heads,
        key_heads,
        value_heads,
        log_total,
        attended,
        normed_two,
        inv_two,
        act_two,
        gelu_slope,
        gelu_half,
    ) = saved
    img_count, seq_len, model_width = cotangent.shape
    head_dim = model_width // HEADS
    score_scale = 1.0 / math.sqrt(head_dim)
    row_count = img_count * seq_len
    head_shape = (img_count, seq_len, HEADS, head_dim)
    vector_float = vector_half.astype(jnp.float32)
    joint_weights = matrix_half[:, : 3 * model_width]
    output_weights = matrix_half[:, 3 * model_width : 4 * model_width]
    upward_weights = matrix_half[:, 4 * model_width :]
    grad_half = cotangent.reshape(row_count, model_width)
    grad_out = grad_half.astype(jnp.float32)
    grad_up = times_transposed(grad_half, down_half) * gelu_slope
    up_half = to_half(grad_up)
    grad_act_two = times_transposed(up_half, upward_weights)
    grad_norm_two, grad_gain_two, grad_shift_two = norm_back(
        grad_act_two, normed_two, inv_two, vector_float[5]
    )
    grad_hidden = grad_out + grad_norm_two
    hidden_half = to_half(grad_hidden)
    grad_att = to_half(times_transposed(hidden_half, output_weights)).reshape(head_shape)
    prob_float = jnp.exp(head_scores(query_heads, key_heads, score_scale) - log_total)
    probs_half = to_half(prob_float)
    grad_probs = jnp.einsum(
        "bqhe,bkhe->bhqk", grad_att, value_heads, preferred_element_type=jnp.float32
    )
    row_inner = jnp.sum(prob_float * grad_probs, axis=-1, keepdims=True)
    grad_scores = to_half(prob_float * (grad_probs - row_inner) * score_scale)
    grad_query = jnp.einsum(
        "bhqk,bkhe->bqhe", grad_scores, key_heads, preferred_element_type=jnp.float32
    ).reshape(row_count, model_width)
    grad_key = jnp.einsum(
        "bhqk,bqhe->bkhe", grad_scores, query_heads, preferred_element_type=jnp.float32
    ).reshape(row_count, model_width)
    grad_value = jnp.einsum(
        "bhqk,bqhe->bkhe", probs_half, grad_att, preferred_element_type=jnp.float32
    ).reshape(row_count, model_width)
    grad_proj = to_half(jnp.concatenate([grad_query, grad_key, grad_value], axis=1))
    grad_act_one = times_transposed(grad_proj, joint_weights)
    grad_norm_one, grad_gain_one, grad_shift_one = norm_back(
        grad_act_one, normed_one, inv_one, vector_float[0]
    )
    input_grad = (grad_hidden + grad_norm_one).reshape(cotangent.shape)
    grad_down = transposed_times(gelu_half, grad_half)
    small_rows = jnp.stack(
        [
            grad_gain_one,
            grad_shift_one,
            jnp.sum(grad_query, axis=0),
            jnp.sum(grad_value, axis=0),
            jnp.sum(grad_hidden, axis=0),
            grad_gain_two,
            grad_shift_two,
            jnp.sum(grad_out, axis=0),
        ]
    )
    grad_vectors = jnp.concatenate(
        [small_rows, jnp.sum(grad_up, axis=0).reshape(4, model_width)], axis=0
    )
    factors = (act_one, grad_proj, attended, hidden_half, act_two, up_half)
    return (input_grad, grad_down, grad_vectors, factors)


def adam_update(weights, first, second, gradient, rate, decay):
    next_first = BETA_ONE * first + (1.0 - BETA_ONE) * gradient
    next_second = BETA_TWO * second + (1.0 - BETA_TWO) * gradient * gradient
    corr_first = next_first / (1.0 - BETA_ONE**STEP_COUNT)
    corr_second = next_second / (1.0 - BETA_TWO**STEP_COUNT)
    updated = weights - rate * (corr_first / (jnp.sqrt(corr_second) + ADAM_EPS) + decay * weights)
    return (updated, next_first, next_second)


def grid_sizes(shards, reps):
    x_size = 1
    while 2 * (2 * x_size) ** 2 <= shards and shards % (2 * x_size) == 0:
        x_size *= 2
    core_size = 2 if reps % 2 == 0 else 1
    return (shards // x_size, x_size, reps // core_size, core_size)


def gather_body(
    sizes, win, wdn, vec, gin, gdn, gvec, local_sem, vec_s, vec_r, *sems
):
    nz, nx, ny, nc = sizes
    shards, reps = nz * nx, ny * nc
    s = lax.axis_index("shard")
    r = lax.axis_index("rep")
    z, x = s // nx, s % nx
    y, c = r // nc, r % nc
    width = win.shape[1] // reps

    def shard_of(kz, kx):
        return lax.rem(z + nz - kz, nz) * nx + lax.rem(x + nx - kx, nx)

    def rep_of(ky):
        return lax.rem(y + ny - ky, ny) * nc + c

    barrier = pltpu.get_barrier_semaphore()
    peers = [(lax.rem(s + k, shards), r) for k in range(1, shards)]
    peers += [(s, lax.rem(y + k, ny) * nc + c) for k in range(1, ny)]
    peers += [(s, y * nc + lax.rem(c + k, nc)) for k in range(1, nc)]
    for ps, pr in peers:
        pl.semaphore_signal(
            barrier,
            inc=1,
            device_id={"shard": ps, "rep": pr},
            device_id_type=pl.DeviceIdType.MESH,
        )
    pl.semaphore_wait(barrier, len(peers))

    started = []

    def send(src, dst, ssem, rsem, ps, pr):
        copy = pltpu.make_async_remote_copy(
            src_ref=src,
            dst_ref=dst,
            send_sem=ssem,
            recv_sem=rsem,
            device_id={"shard": ps, "rep": pr},
            device_id_type=pl.DeviceIdType.MESH,
        )
        copy.start()
        started.append(copy)
        return copy

    def in_slot(kz, kx, ky):
        cols = pl.ds(pl.multiple_of(rep_of(ky) * width, 128), width)
        return gin.at[shard_of(kz, kx), :, cols]

    def dn_slot(kz, kx, ky):
        return gdn.at[shard_of(kz, kx), rep_of(ky)]

    own_cols = pl.ds(pl.multiple_of(r * width, 128), width)
    (zs_i, zr_i, xs_i, xr_i, ys_i, yr_i, cs_i, cr_i) = sems[:8]
    (zs_d, zr_d, xs_d, xr_d, ys_d, yr_d, cs_d, cr_d) = sems[8:]
    mine = [
        pltpu.make_async_copy(win, gin.at[s], local_sem.at[0]),
        pltpu.make_async_copy(wdn, gdn.at[s], local_sem.at[1]),
        pltpu.make_async_copy(vec, gvec.at[s], local_sem.at[2]),
    ]
    vec_copies = [
        send(vec, gvec.at[s], vec_s.at[k], vec_r.at[k], lax.rem(s + k, shards), r)
        for k in range(1, shards)
    ]
    zi, zd = {}, {}
    for k in range(1, nz):
        peer = lax.rem(z + k, nz) * nx + x
        zi[k] = send(
            win.at[:, own_cols], gin.at[s, :, own_cols], zs_i.at[k], zr_i.at[k], peer, r
        )
        zd[k] = send(wdn.at[r], gdn.at[s, r], zs_d.at[k], zr_d.at[k], peer, r)
    xi, xd, yi, yd, ci, cd = {}, {}, {}, {}, {}, {}

    def send_x_in(kz):
        for kx in range(1, nx):
            peer = z * nx + lax.rem(x + kx, nx)
            src = win.at[:, own_cols] if kz == 0 else in_slot(kz, 0, 0)
            xi[kz, kx] = send(
                src, in_slot(kz, 0, 0), xs_i.at[kz, kx], xr_i.at[kz, kx], peer, r
            )

    def send_y_in(kz, kx):
        for ky in range(1, ny):
            peer = lax.rem(y + ky, ny) * nc + c
            slot = in_slot(kz, kx, 0)
            yi[kz, kx, ky] = send(
                slot, slot, ys_i.at[kz, kx, ky], yr_i.at[kz, kx, ky], s, peer
            )

    def send_c_in(kz, kx, ky):
        if nc > 1:
            slot = in_slot(kz, kx, ky)
            ci[kz, kx, ky] = send(
                slot, slot, cs_i.at[kz, kx, ky], cr_i.at[kz, kx, ky], s, y * nc + 1 - c
            )

    def send_y_dn(kz):
        for ky in range(1, ny):
            peer = lax.rem(y + ky, ny) * nc + c
            slot = dn_slot(kz, 0, 0)
            yd[kz, ky] = send(slot, slot, ys_d.at[kz, ky], yr_d.at[kz, ky], s, peer)

    def send_x_dn(kz, ky):
        for kx in range(1, nx):
            peer = z * nx + lax.rem(x + kx, nx)
            src = wdn.at[rep_of(ky)] if kz == 0 else dn_slot(kz, 0, ky)
            xd[kz, kx, ky] = send(
                src,
                dn_slot(kz, 0, ky),
                xs_d.at[kz, kx, ky],
                xr_d.at[kz, kx, ky],
                peer,
                r,
            )

    def send_c_dn(kz, kx, ky):
        if nc > 1:
            slot = dn_slot(kz, kx, ky)
            cd[kz, kx, ky] = send(
                slot, slot, cs_d.at[kz, kx, ky], cr_d.at[kz, kx, ky], s, y * nc + 1 - c
            )

    send_x_in(0)
    for ky in range(ny):
        send_x_dn(0, ky)
    for copy in mine:
        copy.start()
    for kz in range(nz):
        if kz > 0:
            zi[kz].wait_recv()
            send_y_in(kz, 0)
            send_x_in(kz)
            send_c_in(kz, 0, 0)
            zd[kz].wait_recv()
            send_x_dn(kz, 0)
            send_y_dn(kz)
            send_c_dn(kz, 0, 0)
        for kx in range(1, nx):
            xi[kz, kx].wait_recv()
            send_y_in(kz, kx)
            send_c_in(kz, kx, 0)
        if kz > 0:
            for ky in range(1, ny):
                yd[kz, ky].wait_recv()
                send_x_dn(kz, ky)
                send_c_dn(kz, 0, ky)
    for kz in range(nz):
        for kx in range(nx):
            for ky in range(ny):
                if kx > 0:
                    xd[kz, kx, ky].wait_recv()
                    send_c_dn(kz, kx, ky)
                if ky > 0 and (kz > 0 or kx > 0):
                    yi[kz, kx, ky].wait_recv()
                    send_c_in(kz, kx, ky)
    for copy in list(ci.values()) + list(cd.values()) + vec_copies:
        copy.wait_recv()
    for copy in mine:
        copy.wait()
    for copy in started:
        copy.wait_send()


def gather_weights(sizes, win, wdn, vec):
    nz, nx, ny, nc = sizes
    shards, reps = nz * nx, ny * nc
    rows_in, cols_in = win.shape
    rows_dn, cols_dn = wdn.shape
    dma = pltpu.SemaphoreType.DMA
    full = (nz, nx, ny)
    shapes_in = [(nz,), (nz, nx), full, full]
    shapes_dn = [(nz,), full, (nz, ny), full]
    sems = [dma(shape) for shape in shapes_in + shapes_dn for _ in range(2)]

    def body(*refs):
        gather_body(sizes, *refs)

    gin, gdn, gvec = pl.pallas_call(
        body,
        name="gather_weights",
        out_shape=(
            jax.ShapeDtypeStruct((shards, rows_in, cols_in), win.dtype),
            jax.ShapeDtypeStruct((shards, reps, rows_dn // reps, cols_dn), wdn.dtype),
            jax.ShapeDtypeStruct((shards,) + vec.shape, vec.dtype),
        ),
        in_specs=[pl.BlockSpec(memory_space=pltpu.VMEM)] * 3,
        out_specs=[pl.BlockSpec(memory_space=pl.ANY)] * 3,
        scratch_shapes=[dma((3,)), dma((shards,)), dma((shards,))] + sems,
        compiler_params=pltpu.CompilerParams(
            collective_id=0, has_side_effects=True, vmem_limit_bytes=16 << 20
        ),
    )(win, wdn.reshape(reps, rows_dn // reps, cols_dn), vec)
    return (
        gin.reshape(shards * rows_in, cols_in),
        gdn.reshape(shards * rows_dn, cols_dn),
        jnp.swapaxes(gvec, 0, 1).reshape(vec.shape[0], -1),
    )


def axis_info(sizes, name):
    nz, nx, ny, nc = sizes
    s = lax.axis_index("shard")
    r = lax.axis_index("rep")
    position = {"z": 0, "x": 1, "y": 2, "c": 3}[name]
    coordinate = (s // nx, s % nx, r // nc, r % nc)[position]
    size = sizes[position]

    def shift(k):
        pairs = []
        for index in range(nz * nx * ny * nc):
            parts = [
                index // (nc * ny * nx),
                index // (nc * ny) % nx,
                index // nc % ny,
                index % nc,
            ]
            parts[position] = (parts[position] + k) % size
            target = ((parts[0] * nx + parts[1]) * ny + parts[2]) * nc + parts[3]
            pairs.append((index, target))
        return pairs

    return (size, coordinate, shift)


def scatter_axis(sizes, value, name, dim):
    size, me, shift = axis_info(sizes, name)
    take = lambda i: lax.dynamic_index_in_dim(value, i, dim, keepdims=False)
    total = take(me).astype(jnp.float32)
    for k in range(1, size):
        got = lax.ppermute(take(lax.rem(me + k, size)), ("shard", "rep"), shift(k))
        total = total + got.astype(jnp.float32)
    return to_half(total)


def reduce_matrix(sizes, partial, order):
    nz, nx, ny, nc = sizes
    rows, cols = partial.shape
    unit = rows // (nz * nx * ny * nc)
    names = ["z", "x", "y", "c"]
    value = partial.reshape(nz, nx, ny, nc, unit, cols)
    for name in order:
        dim = names.index(name)
        names.pop(dim)
        value = scatter_axis(sizes, value, name, dim)
    reps = ny * nc
    r = lax.axis_index("rep")
    whole = jnp.zeros((reps, unit, cols), value.dtype)
    whole = lax.dynamic_update_index_in_dim(whole, value, r, 0)
    for k in range(1, reps):
        got = lax.ppermute(value, "rep", [(i, (i + k) % reps) for i in range(reps)])
        whole = lax.dynamic_update_index_in_dim(whole, got, lax.rem(r + reps - k, reps), 0)
    return whole.reshape(reps * unit, cols).astype(jnp.float32)


def reduce_small(count, value):
    if count & (count - 1):
        return lax.psum(value, ("shard", "rep"))
    step = 1
    while step < count:
        pairs = [(i, i ^ step) for i in range(count)]
        value = value + lax.ppermute(value, ("shard", "rep"), pairs)
        step *= 2
    return value


def local(
    sizes,
    images,
    cotangent,
    weights_in,
    weights_down,
    vectors,
    mean_in,
    mean_down,
    mean_vectors,
    square_in,
    square_down,
    square_vectors,
):
    halves = (to_half(weights_in), to_half(weights_down), to_half(vectors))
    forward_set = gather_weights(sizes, *halves)
    block_out, saved = forward_pass(images, forward_set[0], forward_set[1], forward_set[2])
    input_grad, grad_down_local, grad_vectors_local, factors = backward_pass(
        cotangent, saved, forward_set[0], forward_set[1], forward_set[2]
    )
    act_one, grad_proj, attended, hidden_half, act_two, up_half = factors

    width = 4 * images.shape[2] // 2
    attention_part = to_half(
        jnp.concatenate(
            [transposed_times(act_one, grad_proj), transposed_times(attended, hidden_half)], axis=1
        )
    )
    up_part = to_half(transposed_times(act_two, up_half))
    down_part = to_half(grad_down_local)
    grad_down = reduce_matrix(sizes, down_part, "cxyz")
    grad_in = jnp.concatenate(
        [
            reduce_matrix(sizes, attention_part[:, :width], "cyxz"),
            reduce_matrix(sizes, attention_part[:, width:], "cxyz"),
            reduce_matrix(sizes, up_part, "cyxz"),
        ],
        axis=1,
    )
    vector_sum = reduce_small(
        sizes[0] * sizes[1] * sizes[2] * sizes[3],
        to_half(grad_vectors_local).astype(jnp.float32),
    )
    owned = vectors.shape[1]
    grad_vectors = lax.dynamic_slice_in_dim(
        vector_sum, lax.axis_index("shard") * owned, owned, axis=1
    )
    new_in = adam_update(weights_in, mean_in, square_in, grad_in, RATE_MATRIX, DECAY_MATRIX)
    new_down = adam_update(
        weights_down, mean_down, square_down, grad_down, RATE_MATRIX, DECAY_MATRIX
    )
    new_vectors = adam_update(vectors, mean_vectors, square_vectors, grad_vectors, RATE_VECTOR, 0.0)
    return (
        block_out,
        input_grad,
        grad_in,
        grad_down,
        grad_vectors,
        new_in[0],
        new_down[0],
        new_vectors[0],
        new_in[1],
        new_down[1],
        new_vectors[1],
        new_in[2],
        new_down[2],
        new_vectors[2],
    )


def solution(mesh):
    placed = (
        P(("shard", "rep"), None, None),
        P(("shard", "rep"), None, None),
        P("shard", None),
        P("shard", None),
        P(None, "shard"),
        P("shard", None),
        P("shard", None),
        P(None, "shard"),
        P("shard", None),
        P("shard", None),
        P(None, "shard"),
    )
    sizes = grid_sizes(mesh.shape["shard"], mesh.shape["rep"])
    return jax.shard_map(
        functools.partial(local, sizes),
        mesh=mesh,
        in_specs=placed,
        out_specs=(
            P(("shard", "rep"), None, None),
            P(("shard", "rep"), None, None),
            P("shard", None),
            P("shard", None),
            P(None, "shard"),
            P("shard", None),
            P("shard", None),
            P(None, "shard"),
            P("shard", None),
            P("shard", None),
            P(None, "shard"),
            P("shard", None),
            P("shard", None),
            P(None, "shard"),
        ),
        check_vma=False,
    )
```

```python
import functools
import math

import jax
import jax.numpy as jnp
from jax import lax
from jax.experimental import pallas as pl
from jax.experimental.pallas import tpu as pltpu
from jax.sharding import PartitionSpec as P

HEADS = 12


NORM_EPS = 1e-06
BETA_ONE = 0.9
BETA_TWO = 0.95
ADAM_EPS = 1e-08
RATE_MATRIX = 0.008
RATE_VECTOR = 0.15
DECAY_MATRIX = 0.05
STEP_COUNT = 2.0


def to_half(array_in):
    return array_in.astype(jnp.bfloat16)


def matmul(left, right):
    return jnp.dot(left, right, preferred_element_type=jnp.float32)


def times_transposed(left, right):
    return lax.dot_general(
        left, right, (((1,), (1,)), ((), ())), preferred_element_type=jnp.float32
    )


def transposed_times(left, right):
    return lax.dot_general(
        left, right, (((0,), (0,)), ((), ())), preferred_element_type=jnp.float32
    )


def layer_norm(inputs, gain, shift):
    centred = inputs - jnp.mean(inputs, axis=-1, keepdims=True)
    inv_std = lax.rsqrt(jnp.mean(centred * centred, axis=-1, keepdims=True) + NORM_EPS)
    normed = centred * inv_std
    return (normed, inv_std, normed * gain + shift)


def norm_back(grad_after, normed, inv_std, gain):
    grad_normed = grad_after * gain
    grad_inputs = inv_std * (
        grad_normed
        - jnp.mean(grad_normed, axis=-1, keepdims=True)
        - normed * jnp.mean(grad_normed * normed, axis=-1, keepdims=True)
    )
    return (grad_inputs, jnp.sum(grad_after * normed, axis=0), jnp.sum(grad_after, axis=0))


def gaussian_unit(hidden):
    cdf_part = 0.5 * (1.0 + jax.scipy.special.erf(hidden * 0.7071067811865476))
    slope = cdf_part + hidden * jnp.exp(-0.5 * hidden * hidden) * 0.3989422804014327
    return (hidden * cdf_part, slope)


def head_scores(query_heads, key_heads, score_scale):
    return (
        jnp.einsum("bqhe,bkhe->bhqk", query_heads, key_heads, preferred_element_type=jnp.float32)
        * score_scale
    )


def forward_pass(images, matrix_half, down_half, vector_half):
    img_count, seq_len, model_width = images.shape
    head_dim = model_width // HEADS
    score_scale = 1.0 / math.sqrt(head_dim)
    row_count = img_count * seq_len
    head_shape = (img_count, seq_len, HEADS, head_dim)
    vector_float = vector_half.astype(jnp.float32)
    flat_in = images.reshape(row_count, model_width).astype(jnp.float32)
    normed_one, inv_one, pre_one = layer_norm(flat_in, vector_float[0], vector_float[1])
    act_one = to_half(pre_one)
    projected = matmul(act_one, matrix_half[:, : 3 * model_width])
    query_heads = to_half(projected[:, :model_width] + vector_float[2]).reshape(head_shape)
    key_heads = to_half(projected[:, model_width : 2 * model_width]).reshape(head_shape)
    value_heads = to_half(projected[:, 2 * model_width :] + vector_float[3]).reshape(head_shape)
    scores = head_scores(query_heads, key_heads, score_scale)
    log_total = jax.nn.logsumexp(scores, axis=-1, keepdims=True)
    probs_half = to_half(jnp.exp(scores - log_total))
    attended = to_half(
        jnp.einsum(
            "bhqk,bkhe->bqhe", probs_half, value_heads, preferred_element_type=jnp.float32
        ).reshape(row_count, model_width)
    )
    hidden_one = (
        flat_in
        + matmul(attended, matrix_half[:, 3 * model_width : 4 * model_width])
        + vector_float[4]
    )
    normed_two, inv_two, pre_two = layer_norm(hidden_one, vector_float[5], vector_float[6])
    act_two = to_half(pre_two)
    up_input = matmul(act_two, matrix_half[:, 4 * model_width :]) + vector_float[8:].reshape(-1)
    gelu_out, gelu_slope = gaussian_unit(up_input)
    gelu_half = to_half(gelu_out)
    block_out = to_half(hidden_one + matmul(gelu_half, down_half) + vector_float[7])
    saved = (
        normed_one,
        inv_one,
        act_one,
        query_heads,
        key_heads,
        value_heads,
        log_total,
        attended,
        normed_two,
        inv_two,
        act_two,
        gelu_slope,
        gelu_half,
    )
    return (block_out.reshape(images.shape), saved)


def backward_pass(cotangent, saved, matrix_half, down_half, vector_half):
    (
        normed_one,
        inv_one,
        act_one,
        query_heads,
        key_heads,
        value_heads,
        log_total,
        attended,
        normed_two,
        inv_two,
        act_two,
        gelu_slope,
        gelu_half,
    ) = saved
    img_count, seq_len, model_width = cotangent.shape
    head_dim = model_width // HEADS
    score_scale = 1.0 / math.sqrt(head_dim)
    row_count = img_count * seq_len
    head_shape = (img_count, seq_len, HEADS, head_dim)
    vector_float = vector_half.astype(jnp.float32)
    joint_weights = matrix_half[:, : 3 * model_width]
    output_weights = matrix_half[:, 3 * model_width : 4 * model_width]
    upward_weights = matrix_half[:, 4 * model_width :]
    grad_half = cotangent.reshape(row_count, model_width)
    grad_out = grad_half.astype(jnp.float32)
    grad_up = times_transposed(grad_half, down_half) * gelu_slope
    up_half = to_half(grad_up)
    grad_act_two = times_transposed(up_half, upward_weights)
    grad_norm_two, grad_gain_two, grad_shift_two = norm_back(
        grad_act_two, normed_two, inv_two, vector_float[5]
    )
    grad_hidden = grad_out + grad_norm_two
    hidden_half = to_half(grad_hidden)
    grad_att = to_half(times_transposed(hidden_half, output_weights)).reshape(head_shape)
    prob_float = jnp.exp(head_scores(query_heads, key_heads, score_scale) - log_total)
    probs_half = to_half(prob_float)
    grad_probs = jnp.einsum(
        "bqhe,bkhe->bhqk", grad_att, value_heads, preferred_element_type=jnp.float32
    )
    row_inner = jnp.sum(prob_float * grad_probs, axis=-1, keepdims=True)
    grad_scores = to_half(prob_float * (grad_probs - row_inner) * score_scale)
    grad_query = jnp.einsum(
        "bhqk,bkhe->bqhe", grad_scores, key_heads, preferred_element_type=jnp.float32
    ).reshape(row_count, model_width)
    grad_key = jnp.einsum(
        "bhqk,bqhe->bkhe", grad_scores, query_heads, preferred_element_type=jnp.float32
    ).reshape(row_count, model_width)
    grad_value = jnp.einsum(
        "bhqk,bqhe->bkhe", probs_half, grad_att, preferred_element_type=jnp.float32
    ).reshape(row_count, model_width)
    grad_proj = to_half(jnp.concatenate([grad_query, grad_key, grad_value], axis=1))
    grad_act_one = times_transposed(grad_proj, joint_weights)
    grad_norm_one, grad_gain_one, grad_shift_one = norm_back(
        grad_act_one, normed_one, inv_one, vector_float[0]
    )
    input_grad = (grad_hidden + grad_norm_one).reshape(cotangent.shape)
    grad_down = transposed_times(gelu_half, grad_half)
    small_rows = jnp.stack(
        [
            grad_gain_one,
            grad_shift_one,
            jnp.sum(grad_query, axis=0),
            jnp.sum(grad_value, axis=0),
            jnp.sum(grad_hidden, axis=0),
            grad_gain_two,
            grad_shift_two,
            jnp.sum(grad_out, axis=0),
        ]
    )
    grad_vectors = jnp.concatenate(
        [small_rows, jnp.sum(grad_up, axis=0).reshape(4, model_width)], axis=0
    )
    factors = (act_one, grad_proj, attended, hidden_half, act_two, up_half)
    return (input_grad, grad_down, grad_vectors, factors)


def adam_update(weights, first, second, gradient, rate, decay):
    next_first = BETA_ONE * first + (1.0 - BETA_ONE) * gradient
    next_second = BETA_TWO * second + (1.0 - BETA_TWO) * gradient * gradient
    corr_first = next_first / (1.0 - BETA_ONE**STEP_COUNT)
    corr_second = next_second / (1.0 - BETA_TWO**STEP_COUNT)
    updated = weights - rate * (corr_first / (jnp.sqrt(corr_second) + ADAM_EPS) + decay * weights)
    return (updated, next_first, next_second)


def grid_sizes(shards, reps):
    x_size = 1
    while 2 * (2 * x_size) ** 2 <= shards and shards % (2 * x_size) == 0:
        x_size *= 2
    core_size = 2 if reps % 2 == 0 else 1
    return (shards // x_size, x_size, reps // core_size, core_size)


def gather_body(
    sizes, win, wdn, vec, gin, gdn, gvec, local_sem, vec_s, vec_r, *sems
):
    nz, nx, ny, nc = sizes
    shards, reps = nz * nx, ny * nc
    s = lax.axis_index("shard")
    r = lax.axis_index("rep")
    z, x = s // nx, s % nx
    y, c = r // nc, r % nc
    width = win.shape[1] // reps

    def shard_of(kz, kx):
        return lax.rem(z + nz - kz, nz) * nx + lax.rem(x + nx - kx, nx)

    def rep_of(ky):
        return lax.rem(y + ny - ky, ny) * nc + c

    barrier = pltpu.get_barrier_semaphore()
    peers = [(lax.rem(s + k, shards), r) for k in range(1, shards)]
    peers += [(s, lax.rem(y + k, ny) * nc + c) for k in range(1, ny)]
    peers += [(s, y * nc + lax.rem(c + k, nc)) for k in range(1, nc)]
    for ps, pr in peers:
        pl.semaphore_signal(
            barrier,
            inc=1,
            device_id={"shard": ps, "rep": pr},
            device_id_type=pl.DeviceIdType.MESH,
        )
    pl.semaphore_wait(barrier, len(peers))

    started = []

    def send(src, dst, ssem, rsem, ps, pr):
        copy = pltpu.make_async_remote_copy(
            src_ref=src,
            dst_ref=dst,
            send_sem=ssem,
            recv_sem=rsem,
            device_id={"shard": ps, "rep": pr},
            device_id_type=pl.DeviceIdType.MESH,
        )
        copy.start()
        started.append(copy)
        return copy

    def in_slot(kz, kx, ky):
        cols = pl.ds(pl.multiple_of(rep_of(ky) * width, 128), width)
        return gin.at[shard_of(kz, kx), :, cols]

    def dn_slot(kz, kx, ky):
        return gdn.at[shard_of(kz, kx), rep_of(ky)]

    own_cols = pl.ds(pl.multiple_of(r * width, 128), width)
    (zs_i, zr_i, xs_i, xr_i, ys_i, yr_i, cs_i, cr_i) = sems[:8]
    (zs_d, zr_d, xs_d, xr_d, ys_d, yr_d, cs_d, cr_d) = sems[8:]
    mine = [
        pltpu.make_async_copy(win, gin.at[s], local_sem.at[0]),
        pltpu.make_async_copy(wdn, gdn.at[s], local_sem.at[1]),
        pltpu.make_async_copy(vec, gvec.at[s], local_sem.at[2]),
    ]
    vec_copies = [
        send(vec, gvec.at[s], vec_s.at[k], vec_r.at[k], lax.rem(s + k, shards), r)
        for k in range(1, shards)
    ]
    zi, zd = {}, {}
    for k in range(1, nz):
        peer = lax.rem(z + k, nz) * nx + x
        zi[k] = send(
            win.at[:, own_cols], gin.at[s, :, own_cols], zs_i.at[k], zr_i.at[k], peer, r
        )
        zd[k] = send(wdn.at[r], gdn.at[s, r], zs_d.at[k], zr_d.at[k], peer, r)
    xi, xd, yi, yd, ci, cd = {}, {}, {}, {}, {}, {}

    def send_x_in(kz):
        for kx in range(1, nx):
            peer = z * nx + lax.rem(x + kx, nx)
            src = win.at[:, own_cols] if kz == 0 else in_slot(kz, 0, 0)
            xi[kz, kx] = send(
                src, in_slot(kz, 0, 0), xs_i.at[kz, kx], xr_i.at[kz, kx], peer, r
            )

    def send_y_in(kz, kx):
        for ky in range(1, ny):
            peer = lax.rem(y + ky, ny) * nc + c
            slot = in_slot(kz, kx, 0)
            yi[kz, kx, ky] = send(
                slot, slot, ys_i.at[kz, kx, ky], yr_i.at[kz, kx, ky], s, peer
            )

    def send_c_in(kz, kx, ky):
        if nc > 1:
            slot = in_slot(kz, kx, ky)
            ci[kz, kx, ky] = send(
                slot, slot, cs_i.at[kz, kx, ky], cr_i.at[kz, kx, ky], s, y * nc + 1 - c
            )

    def send_y_dn(kz):
        for ky in range(1, ny):
            peer = lax.rem(y + ky, ny) * nc + c
            slot = dn_slot(kz, 0, 0)
            yd[kz, ky] = send(slot, slot, ys_d.at[kz, ky], yr_d.at[kz, ky], s, peer)

    def send_x_dn(kz, ky):
        for kx in range(1, nx):
            peer = z * nx + lax.rem(x + kx, nx)
            src = wdn.at[rep_of(ky)] if kz == 0 else dn_slot(kz, 0, ky)
            xd[kz, kx, ky] = send(
                src,
                dn_slot(kz, 0, ky),
                xs_d.at[kz, kx, ky],
                xr_d.at[kz, kx, ky],
                peer,
                r,
            )

    def send_c_dn(kz, kx, ky):
        if nc > 1:
            slot = dn_slot(kz, kx, ky)
            cd[kz, kx, ky] = send(
                slot, slot, cs_d.at[kz, kx, ky], cr_d.at[kz, kx, ky], s, y * nc + 1 - c
            )

    send_x_in(0)
    for ky in range(ny):
        send_x_dn(0, ky)
    for copy in mine:
        copy.start()
    for kz in range(nz):
        if kz > 0:
            zi[kz].wait_recv()
            send_y_in(kz, 0)
            send_x_in(kz)
            send_c_in(kz, 0, 0)
            zd[kz].wait_recv()
            send_x_dn(kz, 0)
            send_y_dn(kz)
            send_c_dn(kz, 0, 0)
        for kx in range(1, nx):
            xi[kz, kx].wait_recv()
            send_y_in(kz, kx)
            send_c_in(kz, kx, 0)
        if kz > 0:
            for ky in range(1, ny):
                yd[kz, ky].wait_recv()
                send_x_dn(kz, ky)
                send_c_dn(kz, 0, ky)
    for kz in range(nz):
        for kx in range(nx):
            for ky in range(ny):
                if kx > 0:
                    xd[kz, kx, ky].wait_recv()
                    send_c_dn(kz, kx, ky)
                if ky > 0 and (kz > 0 or kx > 0):
                    yi[kz, kx, ky].wait_recv()
                    send_c_in(kz, kx, ky)
    for copy in list(ci.values()) + list(cd.values()) + vec_copies:
        copy.wait_recv()
    for copy in mine:
        copy.wait()
    for copy in started:
        copy.wait_send()


def gather_weights(sizes, win, wdn, vec):
    nz, nx, ny, nc = sizes
    shards, reps = nz * nx, ny * nc
    rows_in, cols_in = win.shape
    rows_dn, cols_dn = wdn.shape
    dma = pltpu.SemaphoreType.DMA
    full = (nz, nx, ny)
    shapes_in = [(nz,), (nz, nx), full, full]
    shapes_dn = [(nz,), full, (nz, ny), full]
    sems = [dma(shape) for shape in shapes_in + shapes_dn for _ in range(2)]

    def body(*refs):
        gather_body(sizes, *refs)

    gin, gdn, gvec = pl.pallas_call(
        body,
        name="gather_weights",
        out_shape=(
            jax.ShapeDtypeStruct((shards, rows_in, cols_in), win.dtype),
            jax.ShapeDtypeStruct((shards, reps, rows_dn // reps, cols_dn), wdn.dtype),
            jax.ShapeDtypeStruct((shards,) + vec.shape, vec.dtype),
        ),
        in_specs=[pl.BlockSpec(memory_space=pltpu.VMEM)] * 3,
        out_specs=[pl.BlockSpec(memory_space=pl.ANY)] * 3,
        scratch_shapes=[dma((3,)), dma((shards,)), dma((shards,))] + sems,
        compiler_params=pltpu.CompilerParams(
            collective_id=0, has_side_effects=True, vmem_limit_bytes=16 << 20
        ),
    )(win, wdn.reshape(reps, rows_dn // reps, cols_dn), vec)
    return (
        gin.reshape(shards * rows_in, cols_in),
        gdn.reshape(shards * rows_dn, cols_dn),
        jnp.swapaxes(gvec, 0, 1).reshape(vec.shape[0], -1),
    )


def reduce_body(sizes, orders, *refs):
    nz, nx, ny, nc = sizes
    shards, reps = nz * nx, ny * nc
    count = len(orders)
    s = lax.axis_index("shard")
    r = lax.axis_index("rep")
    place = {"z": s // nx, "x": s % nx, "y": r // nc, "c": r % nc}
    extent = {"z": nz, "x": nx, "y": ny, "c": nc}
    parts, vec = refs[:count], refs[count]
    outs, out_vec = refs[count + 1 : 2 * count + 1], refs[2 * count + 1]
    bufs = refs[2 * count + 2 : 6 * count + 2]
    vec_in, vec_sum, vec_rep = refs[6 * count + 2 : 6 * count + 5]
    send_sem, recv_sem, rep_send, rep_recv, vs_send, vs_recv, vr_send, vr_recv = refs[
        6 * count + 5 :
    ]

    def moved(name, k):
        at = dict(place)
        at[name] = lax.rem(at[name] + k, extent[name])
        return (at["z"] * nx + at["x"], at["y"] * nc + at["c"])

    barrier = pltpu.get_barrier_semaphore()
    peers = [(lax.rem(s + k, shards), r) for k in range(1, shards)]
    peers += [(s, lax.rem(r + k, reps)) for k in range(1, reps)]
    for ps, pr in peers:
        pl.semaphore_signal(
            barrier,
            inc=1,
            device_id={"shard": ps, "rep": pr},
            device_id_type=pl.DeviceIdType.MESH,
        )
    pl.semaphore_wait(barrier, len(peers))
    started = []

    def send(src, dst, ssem, rsem, target):
        copy = pltpu.make_async_remote_copy(
            src_ref=src,
            dst_ref=dst,
            send_sem=ssem,
            recv_sem=rsem,
            device_id={"shard": target[0], "rep": target[1]},
            device_id_type=pl.DeviceIdType.MESH,
        )
        copy.start()
        started.append(copy)
        return copy

    def pick(ref, names, name, i):
        return ref.at[tuple(i if n == name else slice(None) for n in names)]

    flights = {}

    def launch(stream, stage, src):
        order = orders[stream]
        name = order[stage]
        names = [n for n in "zxyc" if n not in order[:stage]]
        buf = bufs[4 * stream + stage]
        flights[stream, stage] = []
        for k in range(1, extent[name]):
            theirs = lax.rem(place[name] + k, extent[name])
            flights[stream, stage].append(
                send(
                    pick(src, names, name, theirs),
                    buf.at[k - 1],
                    send_sem.at[stream, stage, k],
                    recv_sem.at[stream, stage, k],
                    moved(name, k),
                )
            )

    def collect(stream, stage, src, dst):
        order = orders[stream]
        name = order[stage]
        names = [n for n in "zxyc" if n not in order[:stage]]
        rest = [n for n in names if n != name]
        buf = bufs[4 * stream + stage]
        for copy in flights[stream, stage]:
            copy.wait_recv()
        trips = math.prod(extent[n] for n in rest)

        def step(i, carry):
            at, left = {}, i
            for n in reversed(rest):
                at[n] = left % extent[n]
                left = left // extent[n]
            at[name] = place[name]
            index = tuple(at[n] for n in rest)
            total = src[tuple(at[n] for n in names)].astype(jnp.float32)
            for k in range(1, extent[name]):
                total = total + buf[(k - 1,) + index].astype(jnp.float32)
            dst[index] = total.astype(dst.dtype)
            return carry

        if rest:
            lax.fori_loop(0, trips, step, 0)
        else:
            total = src[place[name]].astype(jnp.float32)
            for k in range(1, extent[name]):
                total = total + buf[k - 1].astype(jnp.float32)
            dst[...] = total.astype(dst.dtype)

    for stream in range(count):
        launch(stream, 0, parts[stream])
    vec_flights = [
        send(
            vec.at[lax.rem(s + k, shards)],
            vec_in.at[k - 1],
            vs_send.at[k],
            vs_recv.at[k],
            (lax.rem(s + k, shards), r),
        )
        for k in range(1, shards)
    ]
    for stage in range(3):
        for stream in range(count):
            src = parts[stream] if stage == 0 else bufs[4 * stream + stage - 1].at[0]
            mine = bufs[4 * stream + stage].at[0]
            collect(stream, stage, src, mine)
            launch(stream, stage + 1, mine)
    for copy in vec_flights:
        copy.wait_recv()
    total = vec[s]
    for k in range(1, shards):
        total = total + vec_in[k - 1]
    vec_sum[...] = total
    vec_flights = [
        send(
            vec_sum,
            vec_rep.at[k - 1],
            vr_send.at[k],
            vr_recv.at[k],
            (s, lax.rem(r + k, reps)),
        )
        for k in range(1, reps)
    ]
    last = []
    for stream in range(count):
        mine = outs[stream].at[r]
        collect(stream, 3, bufs[4 * stream + 2].at[0], mine)
        for k in range(1, reps):
            last.append(
                send(
                    mine,
                    mine,
                    rep_send.at[stream, k],
                    rep_recv.at[stream, k],
                    (s, lax.rem(r + k, reps)),
                )
            )
    for copy in vec_flights:
        copy.wait_recv()
    total = vec_sum[...]
    for k in range(1, reps):
        total = total + vec_rep[k - 1]
    out_vec[...] = total
    for copy in last:
        copy.wait_recv()
    for copy in started:
        copy.wait_send()


def reduce_grads(sizes, parts, vec):
    nz, nx, ny, nc = sizes
    extent = {"z": nz, "x": nx, "y": ny, "c": nc}
    shards, reps = nz * nx, ny * nc
    orders = ["cyxz" if i % 2 == 0 else "cxyz" for i in range(len(parts))]
    views, bufs, outs = [], [], []
    for part, order in zip(parts, orders):
        unit, cols = part.shape[0] // (shards * reps), part.shape[1]
        views.append(part.reshape(nz, nx, ny, nc, unit, cols))
        for stage in range(4):
            rest = tuple(extent[n] for n in "zxyc" if n not in order[: stage + 1])
            slots = max(1, extent[order[stage]] - 1)
            bufs.append(pltpu.VMEM((slots,) + rest + (unit, cols), part.dtype))
        outs.append(jax.ShapeDtypeStruct((reps, unit, cols), part.dtype))
    most = max(sizes)
    dma = pltpu.SemaphoreType.DMA
    tile = vec.shape[1:]
    count = len(parts)

    def body(*refs):
        reduce_body(sizes, orders, *refs)

    results = pl.pallas_call(
        body,
        name="reduce_grads",
        out_shape=tuple(outs) + (jax.ShapeDtypeStruct(tile, vec.dtype),),
        in_specs=[pl.BlockSpec(memory_space=pltpu.VMEM)] * (count + 1),
        out_specs=[pl.BlockSpec(memory_space=pltpu.VMEM)] * (count + 1),
        scratch_shapes=bufs
        + [
            pltpu.VMEM((max(1, shards - 1),) + tile, vec.dtype),
            pltpu.VMEM(tile, vec.dtype),
            pltpu.VMEM((max(1, reps - 1),) + tile, vec.dtype),
            dma((count, 4, most)),
            dma((count, 4, most)),
            dma((count, reps)),
            dma((count, reps)),
            dma((shards,)),
            dma((shards,)),
            dma((reps,)),
            dma((reps,)),
        ],
        compiler_params=pltpu.CompilerParams(
            collective_id=1, has_side_effects=True, vmem_limit_bytes=56 << 20
        ),
    )(*views, vec)
    return ([out.reshape(-1, out.shape[2]) for out in results[:count]], results[count])


def axis_info(sizes, name):
    nz, nx, ny, nc = sizes
    s = lax.axis_index("shard")
    r = lax.axis_index("rep")
    position = {"z": 0, "x": 1, "y": 2, "c": 3}[name]
    coordinate = (s // nx, s % nx, r // nc, r % nc)[position]
    size = sizes[position]

    def shift(k):
        pairs = []
        for index in range(nz * nx * ny * nc):
            parts = [
                index // (nc * ny * nx),
                index // (nc * ny) % nx,
                index // nc % ny,
                index % nc,
            ]
            parts[position] = (parts[position] + k) % size
            target = ((parts[0] * nx + parts[1]) * ny + parts[2]) * nc + parts[3]
            pairs.append((index, target))
        return pairs

    return (size, coordinate, shift)


def scatter_axis(sizes, value, name, dim):
    size, me, shift = axis_info(sizes, name)
    take = lambda i: lax.dynamic_index_in_dim(value, i, dim, keepdims=False)
    total = take(me).astype(jnp.float32)
    for k in range(1, size):
        got = lax.ppermute(take(lax.rem(me + k, size)), ("shard", "rep"), shift(k))
        total = total + got.astype(jnp.float32)
    return to_half(total)


def reduce_matrix(sizes, partial, order):
    nz, nx, ny, nc = sizes
    rows, cols = partial.shape
    unit = rows // (nz * nx * ny * nc)
    names = ["z", "x", "y", "c"]
    value = partial.reshape(nz, nx, ny, nc, unit, cols)
    for name in order:
        dim = names.index(name)
        names.pop(dim)
        value = scatter_axis(sizes, value, name, dim)
    reps = ny * nc
    r = lax.axis_index("rep")
    whole = jnp.zeros((reps, unit, cols), value.dtype)
    whole = lax.dynamic_update_index_in_dim(whole, value, r, 0)
    for k in range(1, reps):
        got = lax.ppermute(value, "rep", [(i, (i + k) % reps) for i in range(reps)])
        whole = lax.dynamic_update_index_in_dim(whole, got, lax.rem(r + reps - k, reps), 0)
    return whole.reshape(reps * unit, cols).astype(jnp.float32)


def reduce_small(count, value):
    if count & (count - 1):
        return lax.psum(value, ("shard", "rep"))
    step = 1
    while step < count:
        pairs = [(i, i ^ step) for i in range(count)]
        value = value + lax.ppermute(value, ("shard", "rep"), pairs)
        step *= 2
    return value


def local(
    sizes,
    images,
    cotangent,
    weights_in,
    weights_down,
    vectors,
    mean_in,
    mean_down,
    mean_vectors,
    square_in,
    square_down,
    square_vectors,
):
    halves = (to_half(weights_in), to_half(weights_down), to_half(vectors))
    forward_set = gather_weights(sizes, *halves)
    block_out, saved = forward_pass(images, forward_set[0], forward_set[1], forward_set[2])
    input_grad, grad_down_local, grad_vectors_local, factors = backward_pass(
        cotangent, saved, forward_set[0], forward_set[1], forward_set[2]
    )
    act_one, grad_proj, attended, hidden_half, act_two, up_half = factors

    down_part = to_half(grad_down_local)
    up_part = to_half(transposed_times(act_two, up_half))
    attention_part = to_half(
        jnp.concatenate(
            [transposed_times(act_one, grad_proj), transposed_times(attended, hidden_half)], axis=1
        )
    )
    parts = []
    for part in (up_part, down_part, attention_part):
        half = part.shape[1] // 2
        parts += [part[:, :half], part[:, half:]]
    shards, reps = sizes[0] * sizes[1], sizes[2] * sizes[3]
    owned = vectors.shape[1]
    small = to_half(grad_vectors_local).astype(jnp.float32)
    if weights_in.shape[0] % (8 * reps) == 0 and weights_down.shape[0] % (8 * reps) == 0:
        rows = vectors.shape[0]
        tiles = jnp.swapaxes(small.reshape(rows, shards, owned), 0, 1)
        tiles = jnp.pad(tiles, ((0, 0), (0, -rows % 8), (0, -owned % 128)))
        sums, vector_sum = reduce_grads(sizes, parts, tiles)
        sums = [part.astype(jnp.float32) for part in sums]
        grad_vectors = vector_sum[:rows, :owned]
    else:
        sums = [
            reduce_matrix(sizes, part, "cyxz" if i % 2 == 0 else "cxyz")
            for i, part in enumerate(parts)
        ]
        vector_sum = reduce_small(shards * reps, small)
        grad_vectors = lax.dynamic_slice_in_dim(
            vector_sum, lax.axis_index("shard") * owned, owned, axis=1
        )
    grad_in = jnp.concatenate(sums[4:] + sums[:2], axis=1)
    grad_down = jnp.concatenate(sums[2:4], axis=1)
    new_in = adam_update(weights_in, mean_in, square_in, grad_in, RATE_MATRIX, DECAY_MATRIX)
    new_down = adam_update(
        weights_down, mean_down, square_down, grad_down, RATE_MATRIX, DECAY_MATRIX
    )
    new_vectors = adam_update(vectors, mean_vectors, square_vectors, grad_vectors, RATE_VECTOR, 0.0)
    return (
        block_out,
        input_grad,
        grad_in,
        grad_down,
        grad_vectors,
        new_in[0],
        new_down[0],
        new_vectors[0],
        new_in[1],
        new_down[1],
        new_vectors[1],
        new_in[2],
        new_down[2],
        new_vectors[2],
    )


def solution(mesh):
    placed = (
        P(("shard", "rep"), None, None),
        P(("shard", "rep"), None, None),
        P("shard", None),
        P("shard", None),
        P(None, "shard"),
        P("shard", None),
        P("shard", None),
        P(None, "shard"),
        P("shard", None),
        P("shard", None),
        P(None, "shard"),
    )
    sizes = grid_sizes(mesh.shape["shard"], mesh.shape["rep"])
    return jax.shard_map(
        functools.partial(local, sizes),
        mesh=mesh,
        in_specs=placed,
        out_specs=(
            P(("shard", "rep"), None, None),
            P(("shard", "rep"), None, None),
            P("shard", None),
            P("shard", None),
            P(None, "shard"),
            P("shard", None),
            P("shard", None),
            P(None, "shard"),
            P("shard", None),
            P("shard", None),
            P(None, "shard"),
            P("shard", None),
            P("shard", None),
            P(None, "shard"),
        ),
        check_vma=False,
    )
```

```python
import functools
import math

import jax
import jax.numpy as jnp
from jax import lax
from jax.experimental import pallas as pl
from jax.experimental.pallas import tpu as pltpu
from jax.sharding import PartitionSpec as P

HEADS = 12


NORM_EPS = 1e-06
BETA_ONE = 0.9
BETA_TWO = 0.95
ADAM_EPS = 1e-08
RATE_MATRIX = 0.008
RATE_VECTOR = 0.15
DECAY_MATRIX = 0.05
STEP_COUNT = 2.0


def to_half(array_in):
    return array_in.astype(jnp.bfloat16)


def matmul(left, right):
    return jnp.dot(left, right, preferred_element_type=jnp.float32)


def times_transposed(left, right):
    return lax.dot_general(
        left, right, (((1,), (1,)), ((), ())), preferred_element_type=jnp.float32
    )


def transposed_times(left, right):
    return lax.dot_general(
        left, right, (((0,), (0,)), ((), ())), preferred_element_type=jnp.float32
    )


def layer_norm(inputs, gain, shift):
    centred = inputs - jnp.mean(inputs, axis=-1, keepdims=True)
    inv_std = lax.rsqrt(jnp.mean(centred * centred, axis=-1, keepdims=True) + NORM_EPS)
    normed = centred * inv_std
    return (normed, inv_std, normed * gain + shift)


def norm_back(grad_after, normed, inv_std, gain):
    grad_normed = grad_after * gain
    grad_inputs = inv_std * (
        grad_normed
        - jnp.mean(grad_normed, axis=-1, keepdims=True)
        - normed * jnp.mean(grad_normed * normed, axis=-1, keepdims=True)
    )
    return (grad_inputs, jnp.sum(grad_after * normed, axis=0), jnp.sum(grad_after, axis=0))


def gaussian_unit(hidden):
    cdf_part = 0.5 * (1.0 + jax.scipy.special.erf(hidden * 0.7071067811865476))
    slope = cdf_part + hidden * jnp.exp(-0.5 * hidden * hidden) * 0.3989422804014327
    return (hidden * cdf_part, slope)


def head_scores(query_heads, key_heads, score_scale):
    return (
        jnp.einsum("bqhe,bkhe->bhqk", query_heads, key_heads, preferred_element_type=jnp.float32)
        * score_scale
    )


def forward_pass(images, matrix_half, down_half, vector_half):
    img_count, seq_len, model_width = images.shape
    head_dim = model_width // HEADS
    score_scale = 1.0 / math.sqrt(head_dim)
    row_count = img_count * seq_len
    head_shape = (img_count, seq_len, HEADS, head_dim)
    vector_float = vector_half.astype(jnp.float32)
    flat_in = images.reshape(row_count, model_width).astype(jnp.float32)
    normed_one, inv_one, pre_one = layer_norm(flat_in, vector_float[0], vector_float[1])
    act_one = to_half(pre_one)
    projected = matmul(act_one, matrix_half[:, : 3 * model_width])
    query_heads = to_half(projected[:, :model_width] + vector_float[2]).reshape(head_shape)
    key_heads = to_half(projected[:, model_width : 2 * model_width]).reshape(head_shape)
    value_heads = to_half(projected[:, 2 * model_width :] + vector_float[3]).reshape(head_shape)
    scores = head_scores(query_heads, key_heads, score_scale)
    log_total = jax.nn.logsumexp(scores, axis=-1, keepdims=True)
    probs_half = to_half(jnp.exp(scores - log_total))
    attended = to_half(
        jnp.einsum(
            "bhqk,bkhe->bqhe", probs_half, value_heads, preferred_element_type=jnp.float32
        ).reshape(row_count, model_width)
    )
    hidden_one = (
        flat_in
        + matmul(attended, matrix_half[:, 3 * model_width : 4 * model_width])
        + vector_float[4]
    )
    normed_two, inv_two, pre_two = layer_norm(hidden_one, vector_float[5], vector_float[6])
    act_two = to_half(pre_two)
    up_input = matmul(act_two, matrix_half[:, 4 * model_width :]) + vector_float[8:].reshape(-1)
    gelu_out, gelu_slope = gaussian_unit(up_input)
    gelu_half = to_half(gelu_out)
    block_out = to_half(hidden_one + matmul(gelu_half, down_half) + vector_float[7])
    saved = (
        normed_one,
        inv_one,
        act_one,
        query_heads,
        key_heads,
        value_heads,
        log_total,
        attended,
        normed_two,
        inv_two,
        act_two,
        gelu_slope,
        gelu_half,
    )
    return (block_out.reshape(images.shape), saved)


def backward_pass(cotangent, saved, matrix_half, down_half, vector_half):
    (
        normed_one,
        inv_one,
        act_one,
        query_heads,
        key_heads,
        value_heads,
        log_total,
        attended,
        normed_two,
        inv_two,
        act_two,
        gelu_slope,
        gelu_half,
    ) = saved
    img_count, seq_len, model_width = cotangent.shape
    head_dim = model_width // HEADS
    score_scale = 1.0 / math.sqrt(head_dim)
    row_count = img_count * seq_len
    head_shape = (img_count, seq_len, HEADS, head_dim)
    vector_float = vector_half.astype(jnp.float32)
    joint_weights = matrix_half[:, : 3 * model_width]
    output_weights = matrix_half[:, 3 * model_width : 4 * model_width]
    upward_weights = matrix_half[:, 4 * model_width :]
    grad_half = cotangent.reshape(row_count, model_width)
    grad_out = grad_half.astype(jnp.float32)
    grad_up = times_transposed(grad_half, down_half) * gelu_slope
    up_half = to_half(grad_up)
    grad_act_two = times_transposed(up_half, upward_weights)
    grad_norm_two, grad_gain_two, grad_shift_two = norm_back(
        grad_act_two, normed_two, inv_two, vector_float[5]
    )
    grad_hidden = grad_out + grad_norm_two
    hidden_half = to_half(grad_hidden)
    grad_att = to_half(times_transposed(hidden_half, output_weights)).reshape(head_shape)
    prob_float = jnp.exp(head_scores(query_heads, key_heads, score_scale) - log_total)
    probs_half = to_half(prob_float)
    grad_probs = jnp.einsum(
        "bqhe,bkhe->bhqk", grad_att, value_heads, preferred_element_type=jnp.float32
    )
    row_inner = jnp.sum(prob_float * grad_probs, axis=-1, keepdims=True)
    grad_scores = to_half(prob_float * (grad_probs - row_inner) * score_scale)
    grad_query = jnp.einsum(
        "bhqk,bkhe->bqhe", grad_scores, key_heads, preferred_element_type=jnp.float32
    ).reshape(row_count, model_width)
    grad_key = jnp.einsum(
        "bhqk,bqhe->bkhe", grad_scores, query_heads, preferred_element_type=jnp.float32
    ).reshape(row_count, model_width)
    grad_value = jnp.einsum(
        "bhqk,bqhe->bkhe", probs_half, grad_att, preferred_element_type=jnp.float32
    ).reshape(row_count, model_width)
    grad_proj = to_half(jnp.concatenate([grad_query, grad_key, grad_value], axis=1))
    grad_act_one = times_transposed(grad_proj, joint_weights)
    grad_norm_one, grad_gain_one, grad_shift_one = norm_back(
        grad_act_one, normed_one, inv_one, vector_float[0]
    )
    input_grad = (grad_hidden + grad_norm_one).reshape(cotangent.shape)
    grad_down = transposed_times(gelu_half, grad_half)
    small_rows = jnp.stack(
        [
            grad_gain_one,
            grad_shift_one,
            jnp.sum(grad_query, axis=0),
            jnp.sum(grad_value, axis=0),
            jnp.sum(grad_hidden, axis=0),
            grad_gain_two,
            grad_shift_two,
            jnp.sum(grad_out, axis=0),
        ]
    )
    grad_vectors = jnp.concatenate(
        [small_rows, jnp.sum(grad_up, axis=0).reshape(4, model_width)], axis=0
    )
    factors = (act_one, grad_proj, attended, hidden_half, act_two, up_half)
    return (input_grad, grad_down, grad_vectors, factors)


def adam_update(weights, first, second, gradient, rate, decay):
    next_first = BETA_ONE * first + (1.0 - BETA_ONE) * gradient
    next_second = BETA_TWO * second + (1.0 - BETA_TWO) * gradient * gradient
    corr_first = next_first / (1.0 - BETA_ONE**STEP_COUNT)
    corr_second = next_second / (1.0 - BETA_TWO**STEP_COUNT)
    updated = weights - rate * (corr_first / (jnp.sqrt(corr_second) + ADAM_EPS) + decay * weights)
    return (updated, next_first, next_second)


def grid_sizes(shards, reps):
    x_size = 1
    while 2 * (2 * x_size) ** 2 <= shards and shards % (2 * x_size) == 0:
        x_size *= 2
    core_size = 2 if reps % 2 == 0 else 1
    return (shards // x_size, x_size, reps // core_size, core_size)


def gather_body(
    sizes, win, wdn, vec, gin, gdn, gvec, local_sem, vec_s, vec_r, *sems
):
    nz, nx, ny, nc = sizes
    shards, reps = nz * nx, ny * nc
    s = lax.axis_index("shard")
    r = lax.axis_index("rep")
    z, x = s // nx, s % nx
    y, c = r // nc, r % nc
    width = win.shape[1] // reps

    def shard_of(kz, kx):
        return lax.rem(z + nz - kz, nz) * nx + lax.rem(x + nx - kx, nx)

    def rep_of(ky):
        return lax.rem(y + ny - ky, ny) * nc + c

    barrier = pltpu.get_barrier_semaphore()
    peers = [(lax.rem(s + k, shards), r) for k in range(1, shards)]
    peers += [(s, lax.rem(y + k, ny) * nc + c) for k in range(1, ny)]
    peers += [(s, y * nc + lax.rem(c + k, nc)) for k in range(1, nc)]
    for ps, pr in peers:
        pl.semaphore_signal(
            barrier,
            inc=1,
            device_id={"shard": ps, "rep": pr},
            device_id_type=pl.DeviceIdType.MESH,
        )
    pl.semaphore_wait(barrier, len(peers))

    started = []

    def send(src, dst, ssem, rsem, ps, pr):
        copy = pltpu.make_async_remote_copy(
            src_ref=src,
            dst_ref=dst,
            send_sem=ssem,
            recv_sem=rsem,
            device_id={"shard": ps, "rep": pr},
            device_id_type=pl.DeviceIdType.MESH,
        )
        copy.start()
        started.append(copy)
        return copy

    def in_slot(kz, kx, ky):
        cols = pl.ds(pl.multiple_of(rep_of(ky) * width, 128), width)
        return gin.at[shard_of(kz, kx), :, cols]

    def dn_slot(kz, kx, ky):
        return gdn.at[shard_of(kz, kx), rep_of(ky)]

    own_cols = pl.ds(pl.multiple_of(r * width, 128), width)
    (zs_i, zr_i, xs_i, xr_i, ys_i, yr_i, cs_i, cr_i) = sems[:8]
    (zs_d, zr_d, xs_d, xr_d, ys_d, yr_d, cs_d, cr_d) = sems[8:]
    mine = [
        pltpu.make_async_copy(win, gin.at[s], local_sem.at[0]),
        pltpu.make_async_copy(wdn, gdn.at[s], local_sem.at[1]),
        pltpu.make_async_copy(vec, gvec.at[s], local_sem.at[2]),
    ]
    vec_copies = [
        send(vec, gvec.at[s], vec_s.at[k], vec_r.at[k], lax.rem(s + k, shards), r)
        for k in range(1, shards)
    ]
    zi, zd = {}, {}
    for k in range(1, nz):
        peer = lax.rem(z + k, nz) * nx + x
        zi[k] = send(
            win.at[:, own_cols], gin.at[s, :, own_cols], zs_i.at[k], zr_i.at[k], peer, r
        )
        zd[k] = send(wdn.at[r], gdn.at[s, r], zs_d.at[k], zr_d.at[k], peer, r)
    xi, xd, yi, yd, ci, cd = {}, {}, {}, {}, {}, {}

    def send_x_in(kz):
        for kx in range(1, nx):
            peer = z * nx + lax.rem(x + kx, nx)
            src = win.at[:, own_cols] if kz == 0 else in_slot(kz, 0, 0)
            xi[kz, kx] = send(
                src, in_slot(kz, 0, 0), xs_i.at[kz, kx], xr_i.at[kz, kx], peer, r
            )

    def send_y_in(kz, kx):
        for ky in range(1, ny):
            peer = lax.rem(y + ky, ny) * nc + c
            slot = in_slot(kz, kx, 0)
            yi[kz, kx, ky] = send(
                slot, slot, ys_i.at[kz, kx, ky], yr_i.at[kz, kx, ky], s, peer
            )

    def send_c_in(kz, kx, ky):
        if nc > 1:
            slot = in_slot(kz, kx, ky)
            ci[kz, kx, ky] = send(
                slot, slot, cs_i.at[kz, kx, ky], cr_i.at[kz, kx, ky], s, y * nc + 1 - c
            )

    def send_y_dn(kz):
        for ky in range(1, ny):
            peer = lax.rem(y + ky, ny) * nc + c
            slot = dn_slot(kz, 0, 0)
            yd[kz, ky] = send(slot, slot, ys_d.at[kz, ky], yr_d.at[kz, ky], s, peer)

    def send_x_dn(kz, ky):
        for kx in range(1, nx):
            peer = z * nx + lax.rem(x + kx, nx)
            src = wdn.at[rep_of(ky)] if kz == 0 else dn_slot(kz, 0, ky)
            xd[kz, kx, ky] = send(
                src,
                dn_slot(kz, 0, ky),
                xs_d.at[kz, kx, ky],
                xr_d.at[kz, kx, ky],
                peer,
                r,
            )

    def send_c_dn(kz, kx, ky):
        if nc > 1:
            slot = dn_slot(kz, kx, ky)
            cd[kz, kx, ky] = send(
                slot, slot, cs_d.at[kz, kx, ky], cr_d.at[kz, kx, ky], s, y * nc + 1 - c
            )

    send_x_in(0)
    for ky in range(ny):
        send_x_dn(0, ky)
    for copy in mine:
        copy.start()
    for kz in range(nz):
        if kz > 0:
            zi[kz].wait_recv()
            send_y_in(kz, 0)
            send_x_in(kz)
            send_c_in(kz, 0, 0)
            zd[kz].wait_recv()
            send_x_dn(kz, 0)
            send_y_dn(kz)
            send_c_dn(kz, 0, 0)
        for kx in range(1, nx):
            xi[kz, kx].wait_recv()
            send_y_in(kz, kx)
            send_c_in(kz, kx, 0)
        if kz > 0:
            for ky in range(1, ny):
                yd[kz, ky].wait_recv()
                send_x_dn(kz, ky)
                send_c_dn(kz, 0, ky)
    for kz in range(nz):
        for kx in range(nx):
            for ky in range(ny):
                if kx > 0:
                    xd[kz, kx, ky].wait_recv()
                    send_c_dn(kz, kx, ky)
                if ky > 0 and (kz > 0 or kx > 0):
                    yi[kz, kx, ky].wait_recv()
                    send_c_in(kz, kx, ky)
    for copy in list(ci.values()) + list(cd.values()) + vec_copies:
        copy.wait_recv()
    for copy in mine:
        copy.wait()
    for copy in started:
        copy.wait_send()


def gather_weights(sizes, win, wdn, vec):
    nz, nx, ny, nc = sizes
    shards, reps = nz * nx, ny * nc
    rows_in, cols_in = win.shape
    rows_dn, cols_dn = wdn.shape
    dma = pltpu.SemaphoreType.DMA
    full = (nz, nx, ny)
    shapes_in = [(nz,), (nz, nx), full, full]
    shapes_dn = [(nz,), full, (nz, ny), full]
    sems = [dma(shape) for shape in shapes_in + shapes_dn for _ in range(2)]

    def body(*refs):
        gather_body(sizes, *refs)

    gin, gdn, gvec = pl.pallas_call(
        body,
        name="gather_weights",
        out_shape=(
            jax.ShapeDtypeStruct((shards, rows_in, cols_in), win.dtype),
            jax.ShapeDtypeStruct((shards, reps, rows_dn // reps, cols_dn), wdn.dtype),
            jax.ShapeDtypeStruct((shards,) + vec.shape, vec.dtype),
        ),
        in_specs=[pl.BlockSpec(memory_space=pltpu.VMEM)] * 3,
        out_specs=[pl.BlockSpec(memory_space=pltpu.HBM)] * 3,
        scratch_shapes=[dma((3,)), dma((shards,)), dma((shards,))] + sems,
        compiler_params=pltpu.CompilerParams(
            collective_id=0, has_side_effects=True, vmem_limit_bytes=56 << 20
        ),
    )(win, wdn.reshape(reps, rows_dn // reps, cols_dn), vec)
    return (
        gin.reshape(shards * rows_in, cols_in),
        gdn.reshape(shards * rows_dn, cols_dn),
        jnp.swapaxes(gvec, 0, 1).reshape(vec.shape[0], -1),
    )


def reduce_body(sizes, streams, arrays, *refs):
    nz, nx, ny, nc = sizes
    shards, reps = nz * nx, ny * nc
    count = len(streams)
    orders = [order for _, _, _, order in streams]
    s = lax.axis_index("shard")
    r = lax.axis_index("rep")
    place = {"z": s // nx, "x": s % nx, "y": r // nc, "c": r % nc}
    extent = {"z": nz, "x": nx, "y": ny, "c": nc}
    vec = refs[arrays]
    wholes, out_vec = refs[arrays + 1 : 2 * arrays + 1], refs[2 * arrays + 1]
    parts = [
        refs[array].at[(slice(None),) * 5 + (pl.ds(start, width),)]
        for array, start, width, _ in streams
    ]
    outs = [
        wholes[array].at[:, :, pl.ds(start, width)] for array, start, width, _ in streams
    ]
    base = 2 * arrays + 2
    bufs = refs[base : base + 4 * count]
    vec_in, vec_sum, vec_rep = refs[base + 4 * count : base + 4 * count + 3]
    send_sem, recv_sem, rep_send, rep_recv, vs_send, vs_recv, vr_send, vr_recv = refs[
        base + 4 * count + 3 :
    ]

    def moved(name, k):
        at = dict(place)
        at[name] = lax.rem(at[name] + k, extent[name])
        return (at["z"] * nx + at["x"], at["y"] * nc + at["c"])

    barrier = pltpu.get_barrier_semaphore()
    peers = [(lax.rem(s + k, shards), r) for k in range(1, shards)]
    peers += [(s, lax.rem(r + k, reps)) for k in range(1, reps)]
    for ps, pr in peers:
        pl.semaphore_signal(
            barrier,
            inc=1,
            device_id={"shard": ps, "rep": pr},
            device_id_type=pl.DeviceIdType.MESH,
        )
    pl.semaphore_wait(barrier, len(peers))
    started = []

    def send(src, dst, ssem, rsem, target):
        copy = pltpu.make_async_remote_copy(
            src_ref=src,
            dst_ref=dst,
            send_sem=ssem,
            recv_sem=rsem,
            device_id={"shard": target[0], "rep": target[1]},
            device_id_type=pl.DeviceIdType.MESH,
        )
        copy.start()
        started.append(copy)
        return copy

    def pick(ref, names, name, i):
        return ref.at[tuple(i if n == name else slice(None) for n in names)]

    flights = {}

    def launch(stream, stage, src):
        order = orders[stream]
        name = order[stage]
        names = [n for n in "zxyc" if n not in order[:stage]]
        buf = bufs[4 * stream + stage]
        flights[stream, stage] = []
        for k in range(1, extent[name]):
            theirs = lax.rem(place[name] + k, extent[name])
            flights[stream, stage].append(
                send(
                    pick(src, names, name, theirs),
                    buf.at[k - 1],
                    send_sem.at[stream, stage, k],
                    recv_sem.at[stream, stage, k],
                    moved(name, k),
                )
            )

    def collect(stream, stage, src, dst):
        order = orders[stream]
        name = order[stage]
        names = [n for n in "zxyc" if n not in order[:stage]]
        rest = [n for n in names if n != name]
        buf = bufs[4 * stream + stage]
        for copy in flights[stream, stage]:
            copy.wait_recv()
        trips = math.prod(extent[n] for n in rest)

        def step(i, carry):
            at, left = {}, i
            for n in reversed(rest):
                at[n] = left % extent[n]
                left = left // extent[n]
            at[name] = place[name]
            index = tuple(at[n] for n in rest)
            total = src[tuple(at[n] for n in names)].astype(jnp.float32)
            for k in range(1, extent[name]):
                total = total + buf[(k - 1,) + index].astype(jnp.float32)
            dst[index] = total.astype(dst.dtype)
            return carry

        if rest:
            lax.fori_loop(0, trips, step, 0)
        else:
            total = src[place[name]].astype(jnp.float32)
            for k in range(1, extent[name]):
                total = total + buf[k - 1].astype(jnp.float32)
            dst[...] = total.astype(dst.dtype)

    for stream in range(count):
        launch(stream, 0, parts[stream])
    vec_flights = [
        send(
            vec.at[lax.rem(s + k, shards)],
            vec_in.at[k - 1],
            vs_send.at[k],
            vs_recv.at[k],
            (lax.rem(s + k, shards), r),
        )
        for k in range(1, shards)
    ]
    y, c = place["y"], place["c"]
    across, to_core = {}, []

    def advance(stream, stage):
        src = parts[stream] if stage == 0 else bufs[4 * stream + stage - 1].at[0]
        mine = bufs[4 * stream + stage].at[0] if stage < 3 else outs[stream].at[r]
        collect(stream, stage, src, mine)
        if stage < 3:
            launch(stream, stage + 1, mine)
            return
        for k in range(1, ny):
            across[stream, k] = send(
                mine,
                mine,
                rep_send.at[stream, k],
                rep_recv.at[stream, k],
                (s, lax.rem(y + k, ny) * nc + c),
            )
        share(stream, 0)

    def share(stream, k):
        unit = outs[stream].at[lax.rem(y + ny - k, ny) * nc + c]
        for kc in range(1, nc):
            slot = ny + k * nc + kc
            to_core.append(
                send(
                    unit,
                    unit,
                    rep_send.at[stream, slot],
                    rep_recv.at[stream, slot],
                    (s, y * nc + lax.rem(c + kc, nc)),
                )
            )

    def arrive(stream):
        for k in range(1, ny):
            across[stream, k].wait_recv()
            share(stream, k)

    def sum_vec():
        for copy in vec_flights:
            copy.wait_recv()
        total = vec[s]
        for k in range(1, shards):
            total = total + vec_in[k - 1]
        vec_sum[...] = total
        return [
            send(
                vec_sum,
                vec_rep.at[k - 1],
                vr_send.at[k],
                vr_recv.at[k],
                (s, lax.rem(r + k, reps)),
            )
            for k in range(1, reps)
        ]

    lead = (0.0, 3.5, 7.0, 9.0, 11.0)
    tasks = sorted(
        (lead[stage] + stream * (1.0 if stage == 0 else 1.5), stage, stream)
        for stage in range(5)
        for stream in range(count)
    )
    spread = None
    for _, stage, stream in tasks:
        if stage < 4:
            advance(stream, stage)
        else:
            arrive(stream)
        if stage == 1 and stream == count - 1:
            spread = sum_vec()
    for copy in spread:
        copy.wait_recv()
    total = vec_sum[...]
    for k in range(1, reps):
        total = total + vec_rep[k - 1]
    out_vec[...] = total
    for copy in to_core:
        copy.wait_recv()
    for copy in started:
        copy.wait_send()


def reduce_grads(sizes, parts, vec):
    nz, nx, ny, nc = sizes
    extent = {"z": nz, "x": nx, "y": ny, "c": nc}
    shards, reps = nz * nx, ny * nc
    views, bufs, outs, streams = [], [], [], []
    for array, part in enumerate(parts):
        unit, cols = part.shape[0] // (shards * reps), part.shape[1]
        views.append(part.reshape(nz, nx, ny, nc, unit, cols))
        outs.append(jax.ShapeDtypeStruct((reps, unit, cols), part.dtype))
        pieces = 2 if cols % 256 == 0 and part.size >= 2 * min(part.shape) ** 2 else 1
        for piece in range(pieces):
            order = "cyxz" if pieces == 2 and piece == 0 else "cxyz"
            width = cols // pieces
            streams.append((array, piece * width, width, order))
            for stage in range(4):
                rest = tuple(extent[n] for n in "zxyc" if n not in order[: stage + 1])
                slots = max(1, extent[order[stage]] - 1)
                bufs.append(pltpu.VMEM((slots,) + rest + (unit, width), part.dtype))
    most = max(sizes)
    dma = pltpu.SemaphoreType.DMA
    tile = vec.shape[1:]
    count, arrays = len(streams), len(parts)

    def body(*refs):
        reduce_body(sizes, streams, arrays, *refs)

    results = pl.pallas_call(
        body,
        name="reduce_grads",
        out_shape=tuple(outs) + (jax.ShapeDtypeStruct(tile, vec.dtype),),
        in_specs=[pl.BlockSpec(memory_space=pltpu.VMEM)] * (arrays + 1),
        out_specs=[pl.BlockSpec(memory_space=pltpu.VMEM)] * (arrays + 1),
        scratch_shapes=bufs
        + [
            pltpu.VMEM((max(1, shards - 1),) + tile, vec.dtype),
            pltpu.VMEM(tile, vec.dtype),
            pltpu.VMEM((max(1, reps - 1),) + tile, vec.dtype),
            dma((count, 4, most)),
            dma((count, 4, most)),
            dma((count, ny + reps)),
            dma((count, ny + reps)),
            dma((shards,)),
            dma((shards,)),
            dma((reps,)),
            dma((reps,)),
        ],
        compiler_params=pltpu.CompilerParams(
            collective_id=1, has_side_effects=True, vmem_limit_bytes=56 << 20
        ),
    )(*views, vec)
    return ([out.reshape(-1, out.shape[2]) for out in results[:arrays]], results[arrays])


def axis_info(sizes, name):
    nz, nx, ny, nc = sizes
    s = lax.axis_index("shard")
    r = lax.axis_index("rep")
    position = {"z": 0, "x": 1, "y": 2, "c": 3}[name]
    coordinate = (s // nx, s % nx, r // nc, r % nc)[position]
    size = sizes[position]

    def shift(k):
        pairs = []
        for index in range(nz * nx * ny * nc):
            parts = [
                index // (nc * ny * nx),
                index // (nc * ny) % nx,
                index // nc % ny,
                index % nc,
            ]
            parts[position] = (parts[position] + k) % size
            target = ((parts[0] * nx + parts[1]) * ny + parts[2]) * nc + parts[3]
            pairs.append((index, target))
        return pairs

    return (size, coordinate, shift)


def scatter_axis(sizes, value, name, dim):
    size, me, shift = axis_info(sizes, name)
    take = lambda i: lax.dynamic_index_in_dim(value, i, dim, keepdims=False)
    total = take(me).astype(jnp.float32)
    for k in range(1, size):
        got = lax.ppermute(take(lax.rem(me + k, size)), ("shard", "rep"), shift(k))
        total = total + got.astype(jnp.float32)
    return to_half(total)


def reduce_matrix(sizes, partial, order):
    nz, nx, ny, nc = sizes
    rows, cols = partial.shape
    unit = rows // (nz * nx * ny * nc)
    names = ["z", "x", "y", "c"]
    value = partial.reshape(nz, nx, ny, nc, unit, cols)
    for name in order:
        dim = names.index(name)
        names.pop(dim)
        value = scatter_axis(sizes, value, name, dim)
    reps = ny * nc
    r = lax.axis_index("rep")
    whole = jnp.zeros((reps, unit, cols), value.dtype)
    whole = lax.dynamic_update_index_in_dim(whole, value, r, 0)
    for k in range(1, reps):
        got = lax.ppermute(value, "rep", [(i, (i + k) % reps) for i in range(reps)])
        whole = lax.dynamic_update_index_in_dim(whole, got, lax.rem(r + reps - k, reps), 0)
    return whole.reshape(reps * unit, cols).astype(jnp.float32)


def reduce_small(count, value):
    if count & (count - 1):
        return lax.psum(value, ("shard", "rep"))
    step = 1
    while step < count:
        pairs = [(i, i ^ step) for i in range(count)]
        value = value + lax.ppermute(value, ("shard", "rep"), pairs)
        step *= 2
    return value


def local(
    sizes,
    images,
    cotangent,
    weights_in,
    weights_down,
    vectors,
    mean_in,
    mean_down,
    mean_vectors,
    square_in,
    square_down,
    square_vectors,
):
    halves = (to_half(weights_in), to_half(weights_down), to_half(vectors))
    forward_set = gather_weights(sizes, *halves)
    block_out, saved = forward_pass(images, forward_set[0], forward_set[1], forward_set[2])
    input_grad, grad_down_local, grad_vectors_local, factors = backward_pass(
        cotangent, saved, forward_set[0], forward_set[1], forward_set[2]
    )
    act_one, grad_proj, attended, hidden_half, act_two, up_half = factors

    down_part = to_half(grad_down_local)
    up_part = to_half(transposed_times(act_two, up_half))
    joint_part = to_half(transposed_times(act_one, grad_proj))
    output_part = to_half(transposed_times(attended, hidden_half))
    parts = [up_part, down_part, joint_part, output_part]
    shards, reps = sizes[0] * sizes[1], sizes[2] * sizes[3]
    owned = vectors.shape[1]
    small = to_half(grad_vectors_local).astype(jnp.float32)
    if weights_in.shape[0] % (8 * reps) == 0 and weights_down.shape[0] % (8 * reps) == 0:
        rows = vectors.shape[0]
        tiles = jnp.swapaxes(small.reshape(rows, shards, owned), 0, 1)
        tiles = jnp.pad(tiles, ((0, 0), (0, -rows % 8), (0, -owned % 128)))
        sums, vector_sum = reduce_grads(sizes, parts, tiles)
        sums = [part.astype(jnp.float32) for part in sums]
        grad_vectors = vector_sum[:rows, :owned]
    else:
        sums = [
            reduce_matrix(sizes, part, "cyxz" if i % 2 == 0 else "cxyz")
            for i, part in enumerate(parts)
        ]
        vector_sum = reduce_small(shards * reps, small)
        grad_vectors = lax.dynamic_slice_in_dim(
            vector_sum, lax.axis_index("shard") * owned, owned, axis=1
        )
    grad_in = jnp.concatenate([sums[2], sums[3], sums[0]], axis=1)
    grad_down = sums[1]
    new_in = adam_update(weights_in, mean_in, square_in, grad_in, RATE_MATRIX, DECAY_MATRIX)
    new_down = adam_update(
        weights_down, mean_down, square_down, grad_down, RATE_MATRIX, DECAY_MATRIX
    )
    new_vectors = adam_update(vectors, mean_vectors, square_vectors, grad_vectors, RATE_VECTOR, 0.0)
    return (
        block_out,
        input_grad,
        grad_in,
        grad_down,
        grad_vectors,
        new_in[0],
        new_down[0],
        new_vectors[0],
        new_in[1],
        new_down[1],
        new_vectors[1],
        new_in[2],
        new_down[2],
        new_vectors[2],
    )


def solution(mesh):
    placed = (
        P(("shard", "rep"), None, None),
        P(("shard", "rep"), None, None),
        P("shard", None),
        P("shard", None),
        P(None, "shard"),
        P("shard", None),
        P("shard", None),
        P(None, "shard"),
        P("shard", None),
        P("shard", None),
        P(None, "shard"),
    )
    sizes = grid_sizes(mesh.shape["shard"], mesh.shape["rep"])
    return jax.shard_map(
        functools.partial(local, sizes),
        mesh=mesh,
        in_specs=placed,
        out_specs=(
            P(("shard", "rep"), None, None),
            P(("shard", "rep"), None, None),
            P("shard", None),
            P("shard", None),
            P(None, "shard"),
            P("shard", None),
            P("shard", None),
            P(None, "shard"),
            P("shard", None),
            P("shard", None),
            P(None, "shard"),
            P("shard", None),
            P("shard", None),
            P(None, "shard"),
        ),
        check_vma=False,
    )
```
